128 devices in a mesh: head: 2 (over x_lo), page: 64 (over z, y, x_hi, core).
Axes of the slice: x: 4 (x_hi: 2, x_lo: 2; x = x_hi * 2 + x_lo), y: 4, z: 4, core: 2. Of those that a mesh axis runs over, the one named last changes fastest.
Arguments:
- streams: bfloat16 [32768, 4, 2048], P('page', None, 'head'), may hold values from -90 to 90
- hc_read: float32 [4], replicated, may hold values from 0.1 to 0.6
- hc_carry: float32 [4, 4], replicated, may hold values from -1 to 1
- hc_write: float32 [4], replicated, may hold values from 0.5 to 1.5
- w_qkv: bfloat16 [2048, 3, 2048], P(None, None, 'head'), may hold values from -0.125 to 0.125
- w_out: bfloat16 [2048, 2048], P('head'), may hold values from -0.125 to 0.125
- req_lengths: int32 [64, 4], P('page'), may hold values from 1 to 256, 512 in all within a row
- req_age: int32 [64, 4], P('page'), may hold values from 0 to 384
- cache_order: int32 [64, 12], P('page'), may hold values from 0 to 11, each once within a row
- cache_kv: bfloat16 [768, 2, 128, 2048], P('page', None, None, 'head'), may hold values from -240 to 240
- prefill_kv: bfloat16 [256, 1, 2, 128, 2048], P('page', None, None, None, 'head'), may hold values from -6 to 6
- page_table: int32 [256], P('page'), may hold values from 0 to 511, as said below
Outputs:
- new_streams: bfloat16 [32768, 4, 2048], P('page', None, 'head')
- decode_pages: bfloat16 [512, 1, 2, 128, 2048], P('page', None, None, None, 'head')
The draws below stay inside these ranges and needn't reach their ends.
Inputs may be any that keep to these rules, and one draw needn't show every extreme that they name: `page_table`: distinct values. Block b of page index s goes to owner (s + e) mod 64 with e from 0 to 3; at most 2 blocks of one device go to one owner, and at most 8 blocks to one owner in all; both bounds are reached in every draw.
All inputs are finite; a program needn't handle non-finite values.
Results may differ from the reference program's by a relative error of at most 0.024.
Values may be sent and summed in bfloat16 or wider, within the bound.
No kernel may reach another device: no remote copies, remote signals or barrier semaphores. Data moves between devices by JAX's collectives and lax.ppermute only.
A program may use at most 256 MiB of HBM per device.

```python
import math
import jax
import jax.numpy as jnp
import numpy as np
from jax import lax

D = 2048
NH = 16
HD = 128
NSTREAM = 4
BLOCK = 128
TOK_DEV = 512
REQ_DEV = 4
MAXP = 3
LKV = 1
CAP = 2
REACH = 3
GROUPS = 2
OWNERS = 64
SLOTS = 8
CSLOT = 12
TOKENS = 32768
NPREV = 256


def draw_streams(key, part):
    keys = jax.random.split(key, 3)
    row_scale = jnp.exp(jax.random.uniform(keys[1], (TOKENS, 1, 1), jnp.float32, math.log(0.3), math.log(3.0)))
    column = jnp.arange(D, dtype=jnp.float32) / D
    col_scale = 0.3 * jnp.exp(column * math.log(10.0)) * jnp.exp(jax.random.uniform(keys[2], (D,), jnp.float32, -0.4, 0.4))
    base = jnp.clip(jax.random.normal(keys[0], (TOKENS, NSTREAM, D), jnp.float32), -6.0, 6.0)
    return (base * row_scale * col_scale[None, None, :]).astype(jnp.bfloat16)


def draw_cache_kv(key, part):
    keys = jax.random.split(key, 2)
    shape = (OWNERS * CSLOT, 1, BLOCK, NH * HD)
    key_part = jnp.clip(jax.random.normal(keys[0], shape, jnp.float32), -6.0, 6.0)
    value_part = jnp.clip(jax.random.normal(keys[1], shape, jnp.float32), -6.0, 6.0)
    return jnp.concatenate([key_part, value_part], axis=1).astype(jnp.bfloat16)


def draw_page_table(key, part):
    keys = jax.random.split(key, 5)
    owner_count = OWNERS
    pair_table = jnp.array(np.array([[first_d, second_d] for first_d in range(REACH + 1) for second_d in range(first_d + 1, REACH + 1)], np.int32))
    target = jax.random.randint(keys[0], (), 0, owner_count)
    source = jnp.arange(owner_count, dtype=jnp.int32)
    picked = jax.random.randint(keys[1], (owner_count,), 0, pair_table.shape[0])
    chosen = pair_table[picked]
    behind = (target - source) % owner_count
    partner = jax.random.randint(keys[2], (owner_count,), 0, REACH)
    partner = partner + (partner >= behind).astype(jnp.int32)
    forced = jnp.stack([jnp.minimum(behind, partner), jnp.maximum(behind, partner)], axis=1)
    chosen = jnp.where((behind <= REACH)[:, None], forced, chosen)
    spread = jnp.repeat(chosen, CAP, axis=1)
    shuffle = jax.vmap(lambda row_key: jax.random.permutation(row_key, 2 * CAP))(jax.random.split(keys[3], owner_count))
    distance = jnp.take_along_axis(spread, shuffle.astype(jnp.int32), axis=1)
    owner_idx = ((source[:, None] + distance) % owner_count).reshape(-1)
    block_ids = jnp.arange(owner_idx.shape[0], dtype=jnp.int32)
    rank_in = jnp.sum(((owner_idx[None, :] == owner_idx[:, None]) & (block_ids[None, :] < block_ids[:, None])).astype(jnp.int32), axis=1)
    slot_perm = jax.vmap(lambda row_key: jax.random.permutation(row_key, SLOTS))(jax.random.split(keys[4], owner_count)).astype(jnp.int32)
    slot_idx = slot_perm[owner_idx, rank_in]
    return (owner_idx * SLOTS + slot_idx).astype(jnp.int32)


def plant(values, key, least, largest):
    place = [jax.random.randint(jax.random.fold_in(key, axis), (), 0, length) for axis, length in enumerate(values.shape)]
    longest = values.shape.index(max(values.shape))
    neighbour = place[:longest] + [(place[longest] + 1) % values.shape[longest]] + place[longest + 1:]
    return values.at[tuple(place)].set(least).at[tuple(neighbour)].set(largest)


def block_levels(rng, shape, cuts, least, top_value):
    factor_of = 1.0
    for dim, blocks in cuts:
        draws = jax.random.uniform(jax.random.fold_in(jax.random.fold_in(rng, 6), dim), (blocks,), jnp.float32, least / len(cuts), top_value / len(cuts))
        factor_of = factor_of * jnp.repeat(jnp.exp(draws), shape[dim] // blocks).reshape((-1,) + (1,) * (len(shape) - 1 - dim))
    return factor_of


def profile(amount, total, most, slope):
    loads = [(1 << 20) // math.isqrt(rank ** slope) + 1 for rank in range(2, amount + 1)]
    surplus, given = total - most - (amount - 1), [1] * (amount - 1)
    while surplus > 0:
        movable = [i for i in range(amount - 1) if given[i] < most]
        pool, budget = sum([loads[i] for i in movable]), surplus
        for i in movable:
            more = min(most - given[i], max(1, budget * loads[i] // pool), surplus)
            given[i] = given[i] + more
            surplus = surplus - more
    return np.array([most] + given)


def ragged_sizes(own_key, count, total, bound, skew):
    if count == 2:
        one = jax.random.randint(own_key, (), max(1, total - bound), min(bound, total - 1) + 1)
        return jnp.stack([one, total - one])
    sizes = jnp.asarray(profile(count, total, bound, skew), jnp.int32)
    couples = (count - 1) // 2
    source_of, sink = sizes[1:1 + 2 * couples:2], sizes[2:2 + 2 * couples:2]
    room = jnp.minimum(source_of - 1, bound - sink)
    shifted = jax.random.randint(jax.random.fold_in(own_key, 1), (couples,), 0, 1 << 20) % (room + 1)
    sizes = sizes.at[1:1 + 2 * couples:2].set(source_of - shifted).at[2:2 + 2 * couples:2].set(sink + shifted)
    return sizes[jax.random.permutation(jax.random.fold_in(own_key, 2), count)]


def scatter_about(key, dims, width, most, cuts=(), kind=jnp.bfloat16):
    entries = jax.random.normal(key, dims, jnp.float32) * width
    if len(cuts) > 0:
        entries = block_levels(key, dims, cuts, -0.22, 0.18) * entries
    return jnp.clip(entries, min=-most, max=most).astype(kind)


def setup_inputs(seed: int = 0) -> dict:
    splits = jax.random.split(jax.random.key(seed), 13)
    streams = draw_streams(jax.random.fold_in(splits[12], 71), 0)
    hc_read = jnp.clip(jax.random.uniform(splits[1], (NSTREAM,), jnp.float32, 0.1, 0.6), 0.1, 0.6)
    hc_carry = scatter_about(splits[2], (NSTREAM, NSTREAM), 0.3, 1.0, (), jnp.float32)
    hc_write = jnp.clip(jax.random.uniform(splits[3], (NSTREAM,), jnp.float32, 0.5, 1.5), 0.5, 1.5)
    w_qkv = scatter_about(splits[4], (D, 3, NH * HD), D ** -0.5, 0.125, ((2, 2),))
    w_out = scatter_about(splits[5], (NH * HD, D), (NH * HD) ** -0.5, 0.125, ((0, 2),))
    req_lengths = jax.vmap(lambda own: ragged_sizes(own, REQ_DEV, TOK_DEV, TOK_DEV // 2, 2))(jax.random.split(splits[6], OWNERS)).reshape((OWNERS, REQ_DEV)).astype(jnp.int32)
    req_age = plant(jax.random.randint(splits[7], (OWNERS, REQ_DEV), 0, MAXP * BLOCK + 1), jax.random.fold_in(splits[7], 1), 0, MAXP * BLOCK).astype(jnp.int32)
    cache_order = jax.vmap(lambda own: jax.random.permutation(own, CSLOT))(jax.random.split(splits[8], OWNERS)).reshape((OWNERS, CSLOT)).astype(jnp.int32)
    cache_kv = draw_cache_kv(jax.random.fold_in(splits[12], 71), 0)
    prefill_kv = scatter_about(splits[10], (NPREV, LKV, 2, BLOCK, NH * HD), 1.0, 6.0, ((0, 64), (4, 2)))
    page_table = draw_page_table(jax.random.fold_in(splits[12], 71), 0)
    return dict(streams=streams, hc_read=hc_read, hc_carry=hc_carry, hc_write=hc_write, w_qkv=w_qkv, w_out=w_out, req_lengths=req_lengths, req_age=req_age, cache_order=cache_order, cache_kv=cache_kv, prefill_kv=prefill_kv, page_table=page_table)


EPSILON = 1e-05
ROPE_BASE = 10000.0

def token_positions(lengths, cached_len, token_count):
    req_end = jnp.cumsum(lengths).astype(jnp.int32)
    req_start = req_end - lengths
    token_idx = jnp.arange(token_count, dtype=jnp.int32)
    member = ((token_idx[:, None] >= req_start[None, :]) & (token_idx[:, None] < req_end[None, :])).astype(jnp.int32)
    request = lax.optimization_barrier(jnp.sum(member * jnp.arange(lengths.shape[0], dtype=jnp.int32)[None, :], axis=1))
    offset = token_idx - lax.optimization_barrier(jnp.sum(member * req_start[None, :], axis=1))
    return (request, lax.optimization_barrier(jnp.sum(member * cached_len[None, :], axis=1)) + offset)

def rotary(values, position):
    half_dim = values.shape[-1] // 2
    frequency = ROPE_BASE ** (-2.0 * jnp.arange(half_dim, dtype=jnp.float32) / values.shape[-1])
    angles = position.astype(jnp.float32)[:, None] * frequency[None, :]
    cosine = jnp.cos(angles)[:, None, :]
    sine_part = jnp.sin(angles)[:, None, :]
    first_half = values[..., :half_dim]
    second_half = values[..., half_dim:]
    return jnp.concatenate([first_half * cosine - second_half * sine_part, second_half * cosine + first_half * sine_part], axis=-1)

def attend(queries, key_rows, value_rows, request, cached_kv, slot_order, cached_len, block_rows):
    token_count, head_count, head_dim = queries.shape
    slot_count = cached_kv.shape[0]
    page_len = cached_kv.shape[2]
    per_request = slot_count // cached_len.shape[0]
    slot_ids = jnp.arange(slot_count, dtype=jnp.int32)
    index_of_slot = lax.optimization_barrier(jnp.sum((slot_order[:, None] == slot_ids[None, :]).astype(jnp.int32) * slot_ids[:, None], axis=0))
    slot_request = index_of_slot // per_request
    slot_page = index_of_slot % per_request
    request_ids = jnp.arange(cached_len.shape[0], dtype=jnp.int32)
    slot_age = lax.optimization_barrier(jnp.sum((slot_request[:, None] == request_ids[None, :]).astype(jnp.int32) * cached_len[None, :], axis=1))
    in_page = jnp.arange(page_len, dtype=jnp.int32)
    cache_live = (slot_page[:, None] * page_len + in_page[None, :] < slot_age[:, None]).reshape(-1)
    cache_request = jnp.broadcast_to(slot_request[:, None], (slot_count, page_len)).reshape(-1)
    all_keys = jnp.concatenate([cached_kv[:, 0].reshape(slot_count * page_len, head_count, head_dim), key_rows], axis=0).astype(jnp.float32)
    all_values = jnp.concatenate([cached_kv[:, 1].reshape(slot_count * page_len, head_count, head_dim), value_rows], axis=0).astype(jnp.float32)
    key_request = jnp.concatenate([cache_request, request])
    key_live = jnp.concatenate([cache_live, jnp.ones((token_count,), jnp.bool_)])
    key_order = jnp.concatenate([jnp.full((slot_count * page_len,), -1, jnp.int32), jnp.arange(token_count, dtype=jnp.int32)])
    scaling = 1.0 / math.sqrt(head_dim)

    def one_block(first_row):
        block_query = lax.dynamic_slice_in_dim(queries, first_row, block_rows, 0).astype(jnp.float32)
        block_request = lax.dynamic_slice_in_dim(request, first_row, block_rows, 0)
        position = first_row + jnp.arange(block_rows, dtype=jnp.int32)
        scores = jnp.einsum('qhd,khd->hqk', block_query, all_keys) * scaling
        allowed = (key_request[None, :] == block_request[:, None]) & key_live[None, :] & (key_order[None, :] <= position[:, None])
        scores = jnp.where(allowed[None], scores, -jnp.inf)
        row_max = lax.optimization_barrier(jnp.max(scores, axis=-1, keepdims=True))
        weights = jnp.exp(scores - row_max)
        weights = (weights / lax.optimization_barrier(jnp.sum(weights, axis=-1, keepdims=True))).astype(jnp.bfloat16)
        return jnp.einsum('hqk,khd->qhd', weights.astype(jnp.float32), all_values).astype(jnp.bfloat16)
    starts = jnp.arange(token_count // block_rows, dtype=jnp.int32) * block_rows
    return lax.map(one_block, starts).reshape(token_count, head_count, head_dim)

def reference(streams, hc_read, hc_carry, hc_write, w_qkv, w_out, req_lengths, req_age, cache_order, cache_kv, prefill_kv, page_table):
    wide = streams.astype(jnp.float32)
    mix_input = jnp.einsum('tsd,s->td', wide, hc_read, precision=lax.Precision.HIGHEST)
    row_mean = lax.optimization_barrier(jnp.mean(mix_input, axis=1, keepdims=True))
    centred = mix_input - row_mean
    row_var = lax.optimization_barrier(jnp.mean(centred * centred, axis=1, keepdims=True))
    normed = (centred * lax.rsqrt(row_var + EPSILON)).astype(jnp.bfloat16)
    projected = jnp.dot(normed, w_qkv.reshape(D, 3 * NH * HD), preferred_element_type=jnp.float32)
    projected = projected.reshape(TOKENS, 3, NH, HD)
    request, position = jax.vmap(token_positions, (0, 0, None))(req_lengths, req_age, TOK_DEV)
    position = position.reshape(TOKENS)
    queries = rotary(projected[:, 0], position).astype(jnp.bfloat16)
    key_rows = rotary(projected[:, 1], position).astype(jnp.bfloat16)
    value_rows = projected[:, 2].astype(jnp.bfloat16)
    block_rows = min(512, TOK_DEV)

    def per_owner(pieces):
        return attend(pieces[0], pieces[1], pieces[2], pieces[3], pieces[4], pieces[5], pieces[6], block_rows)
    attended = lax.map(per_owner, (queries.reshape(OWNERS, TOK_DEV, NH, HD), key_rows.reshape(OWNERS, TOK_DEV, NH, HD), value_rows.reshape(OWNERS, TOK_DEV, NH, HD), request, cache_kv.reshape(OWNERS, CSLOT, 2, BLOCK, NH * HD), cache_order, req_age))
    attended = attended.reshape(TOKENS, GROUPS, NH // GROUPS * HD)
    out_rows = w_out.reshape(GROUPS, NH // GROUPS * HD, D)
    update = jnp.zeros((TOKENS, D), jnp.float32)
    for group_idx in range(GROUPS):
        part_out = jnp.dot(attended[:, group_idx], out_rows[group_idx], preferred_element_type=jnp.float32).astype(jnp.bfloat16)
        part_out = lax.optimization_barrier(part_out)
        update = update + part_out.astype(jnp.float32)
    carry = jnp.eye(NSTREAM, dtype=jnp.float32) + hc_carry
    new_streams = jnp.einsum('tid,ij->tjd', wide, carry, precision=lax.Precision.HIGHEST) + hc_write[None, :, None] * update[:, None, :]
    decode_pages = jnp.zeros((OWNERS * SLOTS,) + prefill_kv.shape[1:], jnp.bfloat16).at[page_table].set(prefill_kv)
    return (new_streams.astype(jnp.bfloat16), decode_pages)
```

```python
import math

import jax
import jax.numpy as jnp
from jax import lax
from jax.experimental import pallas as pl
from jax.experimental.pallas import tpu as pltpu
from jax.sharding import PartitionSpec as P

F=jnp.float32; B=jnp.bfloat16
NEG=-1e30
def io(shape,d): return lax.broadcasted_iota(jnp.int32,shape,d)
def dot_t(a,b): return lax.dot_general(a,b,(((1,),(1,)),((),())),preferred_element_type=F)
def dot(a,b): return jnp.dot(a,b,preferred_element_type=F)
QSCALE=math.log2(math.e)/math.sqrt(128.0)

def layer_body(len_ref,age_ref,order_ref,head_ref,own_ref,oth_ref,cos_ref,sin_ref,w_hbm,wo_hbm,kv_hbm,keep_ref,send_ref,
               w,wo,kc,vc,nrm,q,k,v,att,s_ref,p_ref,acc,wsem,wosem,csem):
    h=head_ref[0]
    wcp=[pltpu.make_async_copy(w_hbm.at[c],w.at[c],wsem.at[c]) for c in range(3)]
    for c in wcp: c.start()
    ccp=[]
    for i in range(12):
        pg=order_ref[i]
        ccp.append(pltpu.make_async_copy(kv_hbm.at[pg,0],kc.at[pl.ds(i*128,128),:],csem.at[2*i]))
        ccp.append(pltpu.make_async_copy(kv_hbm.at[pg,1],vc.at[pl.ds(i*128,128),:],csem.at[2*i+1]))
    for c in ccp: c.start()
    wocp=pltpu.make_async_copy(wo_hbm,wo,wosem)
    wocp.start()
    hoff=pl.multiple_of(h*1024,1024); ooff=pl.multiple_of((1-h)*1024,1024)
    def ln(i,_):
        r=pl.ds(pl.multiple_of(i*64,64),64)
        a=own_ref[r,:].astype(F); b=oth_ref[r,:].astype(F)
        m=(jnp.sum(a,axis=1,keepdims=True)+jnp.sum(b,axis=1,keepdims=True))*(1.0/2048)
        a=a-m; b=b-m
        var=(jnp.sum(a*a,axis=1,keepdims=True)+jnp.sum(b*b,axis=1,keepdims=True))*(1.0/2048)
        rs=lax.rsqrt(var+1e-5)
        nrm[r,pl.ds(hoff,1024)]=(a*rs).astype(B)
        nrm[r,pl.ds(ooff,1024)]=(b*rs).astype(B)
        return 0
    lax.fori_loop(0,8,ln,0)
    for c,dst in ((0,q),(1,k),(2,v)):
        wcp[c].wait()
        def proj(i,_,c=c,dst=dst):
            col=pl.ds(pl.multiple_of(i*256,256),256)
            for rb in range(2):
                rows=slice(rb*256,rb*256+256)
                x=dot(nrm[rows,:],w[c,:,col])
                if c<2:
                    co=cos_ref[rows,:]; si=sin_ref[rows,:]
                    y=[]
                    for hh in range(2):
                        xh=x[:,hh*128:hh*128+128]
                        z=xh*co+pltpu.roll(xh,64,1)*si
                        if c==0: z=z*QSCALE
                        y.append(z)
                    x=jnp.concatenate(y,axis=1)
                dst[rows,col]=x.astype(B)
            return 0
        lax.fori_loop(0,4,proj,0)
    for c in ccp: c.wait()
    e=[len_ref[0],len_ref[0]+len_ref[1],len_ref[0]+len_ref[1]+len_ref[2]]
    def tile(t,_):
        t0=t*128
        rows=pl.ds(pl.multiple_of(t0,128),128)
        kb=jnp.maximum(t-2,0)*128
        win=pl.ds(pl.multiple_of(kb,128),384)
        ri=t0+io((128,384),0); ki=kb+io((128,384),1)
        st=jnp.where(ri>=e[2],e[2],jnp.where(ri>=e[1],e[1],jnp.where(ri>=e[0],e[0],0)))
        bias=jnp.where((ki>=st)&(ki<=ri),0.0,NEG)
        for hh in range(8):
            hs=slice(hh*128,hh*128+128)
            s_ref[hh,:,384:768]=dot_t(q[rows,hs],k[win,hs])+bias
        rid=t0+io((128,1),0)
        rreq=(rid>=e[0]).astype(jnp.int32)+(rid>=e[1]).astype(jnp.int32)+(rid>=e[2]).astype(jnp.int32)
        last=t0+127
        lo=(t0>=e[0]).astype(jnp.int32)+(t0>=e[1]).astype(jnp.int32)+(t0>=e[2]).astype(jnp.int32)
        hi=(last>=e[0]).astype(jnp.int32)+(last>=e[1]).astype(jnp.int32)+(last>=e[2]).astype(jnp.int32)
        def sc(r,_):
            cb=jnp.where(io((1,384),1)<age_ref[r],0.0,NEG)
            keys=pl.ds(pl.multiple_of(r*384,384),384)
            mine=rreq==r
            for hh in range(8):
                hs=slice(hh*128,hh*128+128)
                x=dot_t(q[rows,hs],kc[keys,hs])+cb
                s_ref[hh,:,0:384]=jnp.where(mine,x,s_ref[hh,:,0:384])
            return 0
        lax.fori_loop(lo,hi+1,sc,0)
        for hh in range(8):
            hs=slice(hh*128,hh*128+128)
            s=s_ref[hh]
            m=jnp.max(s,axis=1,keepdims=True)
            p=jnp.exp2(s-m)
            l=jnp.sum(p,axis=1,keepdims=True)
            p=(p*(1.0/l)).astype(B)
            p_ref[hh]=p[:,0:384]
            acc[:,hs]=dot(p[:,384:768],v[win,hs])
        def pv(r,_):
            keys=pl.ds(pl.multiple_of(r*384,384),384)
            mine=rreq==r
            for hh in range(8):
                hs=slice(hh*128,hh*128+128)
                pm=jnp.where(mine,p_ref[hh],jnp.zeros((),B))
                acc[:,hs]=acc[:,hs]+dot(pm,vc[keys,hs])
            return 0
        lax.fori_loop(lo,hi+1,pv,0)
        att[rows,:]=acc[...].astype(B)
        return 0
    lax.fori_loop(0,4,tile,0)
    wocp.wait()
    def outp(i,_):
        lc=pl.multiple_of(i*256,256)
        for dst,off in ((send_ref,ooff),(keep_ref,hoff)):
            col=pl.ds(pl.multiple_of(off+lc,256),256)
            for rb in range(2):
                rows=slice(rb*256,rb*256+256)
                dst[rows,pl.ds(lc,256)]=dot(att[rows,:],wo[:,col]).astype(B)
        return 0
    lax.fori_loop(0,4,outp,0)

def layer(lens,age,order,head,own,oth,cos,sin,w3,wo,kv):
    vm=pl.BlockSpec(memory_space=pltpu.VMEM); an=pl.BlockSpec(memory_space=pl.ANY); sm=pl.BlockSpec(memory_space=pltpu.SMEM)
    return pl.pallas_call(layer_body,
        out_shape=(jax.ShapeDtypeStruct((512,1024),B),)*2,
        in_specs=[sm]*4+[vm]*4+[an]*3, out_specs=(vm,vm),
        scratch_shapes=[pltpu.VMEM((3,2048,1024),B),pltpu.VMEM((1024,2048),B),pltpu.VMEM((1536,1024),B),pltpu.VMEM((1536,1024),B),
            pltpu.VMEM((512,2048),B),pltpu.VMEM((512,1024),B),pltpu.VMEM((512,1024),B),pltpu.VMEM((512,1024),B),pltpu.VMEM((512,1024),B),
            pltpu.VMEM((8,128,768),F),pltpu.VMEM((8,128,384),B),pltpu.VMEM((128,1024),F),
            pltpu.SemaphoreType.DMA((3,)),pltpu.SemaphoreType.DMA,pltpu.SemaphoreType.DMA((24,))],
        compiler_params=pltpu.CompilerParams(vmem_limit_bytes=60<<20),
        cost_estimate=pl.CostEstimate(flops=14*10**9,bytes_accessed=26<<20,transcendentals=4<<20),
        name='layer')(lens,age,order,head,own,oth,cos,sin,w3,wo,kv)

def tables(lens,age):
    ends=jnp.cumsum(lens); starts=ends-lens
    t=jnp.arange(512,dtype=jnp.int32)
    mem=((t[:,None]>=starts[None,:])&(t[:,None]<ends[None,:])).astype(jnp.int32)
    pos=t+jnp.sum(mem*(age-starts)[None,:],axis=1)
    j=jnp.arange(128,dtype=jnp.int32)
    freq=10000.0**(-2.0*(j%64).astype(F)/128)
    ang=pos.astype(F)[:,None]*freq[None,:]
    return jnp.cos(ang), jnp.where(j[None,:]<64,-1.0,1.0)*jnp.sin(ang)

def rows_view(x):
    return x.reshape(512,4,8,128).transpose(0,2,1,3).reshape(16384,128)

def rows_unview(x):
    return x.reshape(512,8,4,128).transpose(0,2,1,3).reshape(512,4,1024)

NCH=8
TCH=512//NCH

def mix_body(r_ref,x_hbm,o_ref,x,sem):
    cps=[pltpu.make_async_copy(x_hbm.at[pl.ds(c*TCH*32,TCH*32),:],x.at[pl.ds(c*TCH*32,TCH*32),:],sem.at[c]) for c in range(NCH)]
    for c in cps: c.start()
    sh=(64,256); row=io(sh,0); col=io(sh,1)
    c=col&3
    a=jnp.where(c==0,r_ref[0],jnp.where(c==1,r_ref[1],jnp.where(c==2,r_ref[2],r_ref[3])))
    a=jnp.where(((col>>5)==(row&7))&(((col>>2)&7)==(row>>3)),a,0.0)
    hi=a.astype(B)
    A=jnp.concatenate([hi,(a-hi.astype(F)).astype(B)],axis=0)
    for ch in range(NCH):
        cps[ch].wait()
        for g in range(ch*TCH//16,(ch+1)*TCH//16):
            X=jnp.concatenate([x[g*512:g*512+256,:],x[g*512+256:g*512+512,:]],axis=1)
            o=dot(A,X)
            o=o[0:64]+o[64:128]
            for j in range(8):
                o_ref[g*16:g*16+16,j*128:(j+1)*128]=jnp.concatenate([o[j*8:j*8+8,0:128],o[j*8:j*8+8,128:256]],axis=0).astype(B)

def mix(x,r):
    return pl.pallas_call(mix_body,out_shape=jax.ShapeDtypeStruct((512,1024),B),
      in_specs=[pl.BlockSpec(memory_space=pltpu.SMEM),pl.BlockSpec(memory_space=pl.ANY)],
      out_specs=pl.BlockSpec(memory_space=pltpu.VMEM),
      scratch_shapes=[pltpu.VMEM((16384,128),B),pltpu.SemaphoreType.DMA((NCH,))],
      compiler_params=pltpu.CompilerParams(vmem_limit_bytes=60<<20),
      cost_estimate=pl.CostEstimate(flops=10**8,bytes_accessed=6<<20,transcendentals=0),
      name='mix')(r,x)

def fin_body(c_ref,w_ref,x_hbm,a_ref,b_ref,o_hbm,x,o,m_ref,wm_ref,isem,osem):
    icp=[pltpu.make_async_copy(x_hbm.at[pl.ds(c*TCH*32,TCH*32),:],x.at[pl.ds(c*TCH*32,TCH*32),:],isem.at[c]) for c in range(NCH)]
    ocp=[pltpu.make_async_copy(o.at[pl.ds(c*TCH*32,TCH*32),:],o_hbm.at[pl.ds(c*TCH*32,TCH*32),:],osem.at[c]) for c in range(NCH)]
    for c in icp: c.start()
    n=128
    row=io((n,n),0); col=io((n,n),1)
    a=jnp.zeros((n,n),F)
    for i in range(4):
        for j in range(4):
            a=jnp.where(((row&3)==j)&((col&3)==i),c_ref[i*4+j],a)
    a=jnp.where((row>>2)==(col>>2),a,0.0)
    hi=a.astype(B); m_ref[:,0:n]=hi; m_ref[:,n:2*n]=(a-hi.astype(F)).astype(B)
    for s in range(2):
        row=io((n,64),0); col=io((n,64),1)
        a=jnp.zeros((n,64),F)
        for j in range(4): a=jnp.where((row&3)==j,w_ref[j],a)
        a=jnp.where(((row>>5)+s*4==(col&7))&(((row>>2)&7)==(col>>3)),a,0.0)
        hi=a.astype(B); lo=(a-hi.astype(F)).astype(B)
        wm_ref[s*n:(s+1)*n,:]=jnp.concatenate([hi,lo,hi,lo],axis=1)
    M=m_ref[...]
    for ch in range(NCH):
        icp[ch].wait()
        for g in range(ch*TCH//16,(ch+1)*TCH//16):
            def U(ref):
                u=ref[g*16:g*16+16,:].astype(F)
                return jnp.concatenate([jnp.concatenate([u[0:8,j*128:(j+1)*128],u[8:16,j*128:(j+1)*128]],axis=1) for j in range(8)],axis=0).astype(B)
            Ua=U(a_ref);Ub=U(b_ref)
            ou=dot(wm_ref[...],jnp.concatenate([Ua,Ua,Ub,Ub],axis=0))
            r0=g*512
            for s in range(2):
                X=jnp.concatenate([x[r0+s*128:r0+s*128+128,:],x[r0+256+s*128:r0+256+s*128+128,:]],axis=1)
                z=(dot(M,jnp.concatenate([X,X],axis=0))+ou[s*128:(s+1)*128]).astype(B)
                o[r0+s*128:r0+s*128+128,:]=z[:,0:128]; o[r0+256+s*128:r0+256+s*128+128,:]=z[:,128:256]
        ocp[ch].start()
    for c in ocp: c.wait()

def fin(x,u1,u2,cr,w):
    vm=pl.BlockSpec(memory_space=pltpu.VMEM); an=pl.BlockSpec(memory_space=pl.ANY); sm=pl.BlockSpec(memory_space=pltpu.SMEM)
    return pl.pallas_call(fin_body,out_shape=jax.ShapeDtypeStruct((16384,128),B),
      in_specs=[sm,sm,an,vm,vm],out_specs=an,
      scratch_shapes=[pltpu.VMEM((16384,128),B),pltpu.VMEM((16384,128),B),pltpu.VMEM((128,256),B),pltpu.VMEM((256,256),B),
        pltpu.SemaphoreType.DMA((NCH,)),pltpu.SemaphoreType.DMA((NCH,))],
      compiler_params=pltpu.CompilerParams(vmem_limit_bytes=60<<20),
      cost_estimate=pl.CostEstimate(flops=10**9,bytes_accessed=10<<20,transcendentals=0),
      name='fin')(cr,w,x,u1,u2)

def pick_body(tab_ref,me_ref,src,o1,o2,o3,sem):
    me=me_ref[0]
    cps=[]
    for d,dst in ((1,o1),(2,o2),(3,o3)):
        cnt=jnp.int32(0); first=jnp.int32(0); second=jnp.int32(0)
        for b in range(4):
            hit=(((tab_ref[b]>>3)-me)&63)==d
            first=jnp.where(hit&(cnt==0),b,first)
            second=jnp.where(hit&(cnt==1),b,second)
            cnt=cnt+hit.astype(jnp.int32)
        for s,i in ((0,first),(1,second)):
            c=pltpu.make_async_copy(src.at[i],dst.at[s],sem.at[2*(d-1)+s]); c.start(); cps.append(c)
    for c in cps: c.wait()

def pick(tab,me,pre):
    an=pl.BlockSpec(memory_space=pl.ANY); sm=pl.BlockSpec(memory_space=pltpu.SMEM)
    return pl.pallas_call(pick_body,out_shape=(jax.ShapeDtypeStruct((2,2,128,1024),B),)*3,
      in_specs=[sm,sm,an],out_specs=(an,)*3,scratch_shapes=[pltpu.SemaphoreType.DMA((6,))],
      compiler_params=pltpu.CompilerParams(vmem_limit_bytes=60<<20),
      cost_estimate=pl.CostEstimate(flops=0,bytes_accessed=6<<20,transcendentals=0),
      name='pick')(tab,me,pre)

def place_body(t0,t1,t2,t3,me_ref,src,r1,r2,r3,out,zero,sem):
    me=me_ref[0]
    zero[...]=jnp.zeros_like(zero)
    used=jnp.int32(0)
    for tab,ref,own in ((t0,src,True),(t1,r1,False),(t2,r2,False),(t3,r3,False)):
        cnt=jnp.int32(0)
        for b in range(4):
            v=tab[b]
            hit=(v>>3)==me
            slot=v&7
            i=b if own else jnp.minimum(cnt,1)
            @pl.when(hit)
            def _(ref=ref,i=i,slot=slot):
                pltpu.make_async_copy(ref.at[i],out.at[slot],sem.at[slot]).start()
            cnt=cnt+hit.astype(jnp.int32)
            used=used|jnp.where(hit,jnp.int32(1)<<slot,0)
    for s in range(8):
        @pl.when(((used>>s)&1)==0)
        def _(s=s):
            pltpu.make_async_copy(zero,out.at[s],sem.at[s]).start()
    for s in range(8):
        pltpu.make_async_copy(zero,out.at[s],sem.at[s]).wait()

def place(tabs,me,pre,r1,r2,r3):
    an=pl.BlockSpec(memory_space=pl.ANY); sm=pl.BlockSpec(memory_space=pltpu.SMEM)
    return pl.pallas_call(place_body,out_shape=jax.ShapeDtypeStruct((8,2,128,1024),B),
      in_specs=[sm]*5+[an]*4,out_specs=an,
      scratch_shapes=[pltpu.VMEM((2,128,1024),B),pltpu.SemaphoreType.DMA((8,))],
      compiler_params=pltpu.CompilerParams(vmem_limit_bytes=60<<20),
      cost_estimate=pl.CostEstimate(flops=0,bytes_accessed=8<<20,transcendentals=0),
      name='place')(*tabs,me,pre,r1,r2,r3)

def ahead(value,steps):
    return lax.ppermute(value,"page",[(s,(s+steps)%64) for s in range(64)])

def swap(value):
    return lax.ppermute(value,"head",[(0,1),(1,0)])

def body(streams,hc_read,hc_carry,hc_write,w_qkv,w_out,req_lengths,req_age,cache_order,cache_kv,prefill_kv,page_table):
    head=lax.axis_index("head").astype(jnp.int32).reshape(1)
    me=lax.axis_index("page").astype(jnp.int32).reshape(1)
    lens=req_lengths[0]; age=req_age[0]; order=cache_order[0]
    x=rows_view(streams)
    own=mix(x,hc_read)
    oth=swap(own)
    pre=prefill_kv.reshape(4,2,128,1024)
    table=page_table
    own_dep,table_dep=lax.optimization_barrier((own,table))
    s1,s2,s3=pick(table_dep,me,pre)
    r1=ahead(s1,1); r2=ahead(s2,2); r3=ahead(s3,3)
    tabs=(table,ahead(table,1),ahead(table,2),ahead(table,3))
    cos,sin=tables(lens,age)
    oth,tabs=lax.optimization_barrier((oth,tabs))
    w3=w_qkv.transpose(1,0,2)
    keep,send=layer(lens,age,order,head,own,oth,cos,sin,w3,w_out,cache_kv)
    recv=swap(send)
    pages=place(tabs,me,pre,r1,r2,r3)
    carry=(jnp.eye(4,dtype=F)+hc_carry).reshape(16)
    new=fin(x,keep,recv,carry,hc_write)
    return rows_unview(new),pages.reshape(8,1,2,128,1024)

def solution(mesh):
    placed=(P("page",None,"head"),P(),P(),P(),P(None,None,"head"),P("head",None),P("page",None),P("page",None),P("page",None),
        P("page",None,None,"head"),P("page",None,None,None,"head"),P("page"))
    return jax.shard_map(body,mesh=mesh,in_specs=placed,out_specs=(P("page",None,"head"),P("page",None,None,None,"head")),check_vma=False)
```

```python
import math

import jax
import jax.numpy as jnp
from jax import lax
from jax.experimental import pallas as pl
from jax.experimental.pallas import tpu as pltpu
from jax.sharding import PartitionSpec as P

F=jnp.float32; B=jnp.bfloat16
NEG=-1e30
def io(shape,d): return lax.broadcasted_iota(jnp.int32,shape,d)
def dot_t(a,b): return lax.dot_general(a,b,(((1,),(1,)),((),())),preferred_element_type=F)
def dot(a,b): return jnp.dot(a,b,preferred_element_type=F)
QSCALE=math.log2(math.e)/math.sqrt(128.0)

def layer_body(len_ref,age_ref,order_ref,head_ref,own_ref,oth_ref,cos_ref,sin_ref,w_hbm,wo_hbm,kv_hbm,keep_ref,send_ref,
               w,wo,kc,vc,nrm,q,k,v,att,s_ref,p_ref,acc,wsem,wosem,csem):
    h=head_ref[0]
    wcp=[pltpu.make_async_copy(w_hbm.at[c],w.at[c],wsem.at[c]) for c in range(3)]
    for c in wcp: c.start()
    ccp=[]
    for i in range(12):
        pg=order_ref[i]
        ccp.append(pltpu.make_async_copy(kv_hbm.at[pg,0],kc.at[pl.ds(i*128,128),:],csem.at[2*i]))
        ccp.append(pltpu.make_async_copy(kv_hbm.at[pg,1],vc.at[pl.ds(i*128,128),:],csem.at[2*i+1]))
    for c in ccp: c.start()
    wocp=pltpu.make_async_copy(wo_hbm,wo,wosem)
    wocp.start()
    hoff=pl.multiple_of(h*1024,1024); ooff=pl.multiple_of((1-h)*1024,1024)
    def ln(i,_):
        r=pl.ds(pl.multiple_of(i*64,64),64)
        a=own_ref[r,:].astype(F); b=oth_ref[r,:].astype(F)
        m=(jnp.sum(a,axis=1,keepdims=True)+jnp.sum(b,axis=1,keepdims=True))*(1.0/2048)
        a=a-m; b=b-m
        var=(jnp.sum(a*a,axis=1,keepdims=True)+jnp.sum(b*b,axis=1,keepdims=True))*(1.0/2048)
        rs=lax.rsqrt(var+1e-5)
        nrm[r,pl.ds(hoff,1024)]=(a*rs).astype(B)
        nrm[r,pl.ds(ooff,1024)]=(b*rs).astype(B)
        return 0
    lax.fori_loop(0,8,ln,0)
    for c,dst in ((0,q),(1,k),(2,v)):
        wcp[c].wait()
        def proj(i,_,c=c,dst=dst):
            col=pl.ds(pl.multiple_of(i*256,256),256)
            for rb in range(2):
                rows=slice(rb*256,rb*256+256)
                x=dot(nrm[rows,:],w[c,:,col])
                if c<2:
                    co=cos_ref[rows,:]; si=sin_ref[rows,:]
                    y=[]
                    for hh in range(2):
                        xh=x[:,hh*128:hh*128+128]
                        z=xh*co+pltpu.roll(xh,64,1)*si
                        if c==0: z=z*QSCALE
                        y.append(z)
                    x=jnp.concatenate(y,axis=1)
                dst[rows,col]=x.astype(B)
            return 0
        lax.fori_loop(0,4,proj,0)
    for c in ccp: c.wait()
    e=[len_ref[0],len_ref[0]+len_ref[1],len_ref[0]+len_ref[1]+len_ref[2]]
    def tile(t,_):
        t0=t*128
        rows=pl.ds(pl.multiple_of(t0,128),128)
        kb=jnp.maximum(t-2,0)*128
        win=pl.ds(pl.multiple_of(kb,128),384)
        ri=t0+io((128,384),0); ki=kb+io((128,384),1)
        st=jnp.where(ri>=e[2],e[2],jnp.where(ri>=e[1],e[1],jnp.where(ri>=e[0],e[0],0)))
        bias=jnp.where((ki>=st)&(ki<=ri),0.0,NEG)
        for hh in range(8):
            hs=slice(hh*128,hh*128+128)
            s_ref[hh,:,384:768]=dot_t(q[rows,hs],k[win,hs])+bias
        rid=t0+io((128,1),0)
        rreq=(rid>=e[0]).astype(jnp.int32)+(rid>=e[1]).astype(jnp.int32)+(rid>=e[2]).astype(jnp.int32)
        last=t0+127
        lo=(t0>=e[0]).astype(jnp.int32)+(t0>=e[1]).astype(jnp.int32)+(t0>=e[2]).astype(jnp.int32)
        hi=(last>=e[0]).astype(jnp.int32)+(last>=e[1]).astype(jnp.int32)+(last>=e[2]).astype(jnp.int32)
        def sc(r,_):
            cb=jnp.where(io((1,384),1)<age_ref[r],0.0,NEG)
            keys=pl.ds(pl.multiple_of(r*384,384),384)
            mine=rreq==r
            for hh in range(8):
                hs=slice(hh*128,hh*128+128)
                x=dot_t(q[rows,hs],kc[keys,hs])+cb
                s_ref[hh,:,0:384]=jnp.where(mine,x,s_ref[hh,:,0:384])
            return 0
        lax.fori_loop(lo,hi+1,sc,0)
        for hh in range(8):
            hs=slice(hh*128,hh*128+128)
            s=s_ref[hh]
            m=jnp.max(s,axis=1,keepdims=True)
            p=jnp.exp2(s-m)
            l=jnp.sum(p,axis=1,keepdims=True)
            p=(p*(1.0/l)).astype(B)
            p_ref[hh]=p[:,0:384]
            acc[:,hs]=dot(p[:,384:768],v[win,hs])
        def pv(r,_):
            keys=pl.ds(pl.multiple_of(r*384,384),384)
            mine=rreq==r
            for hh in range(8):
                hs=slice(hh*128,hh*128+128)
                pm=jnp.where(mine,p_ref[hh],jnp.zeros((),B))
                acc[:,hs]=acc[:,hs]+dot(pm,vc[keys,hs])
            return 0
        lax.fori_loop(lo,hi+1,pv,0)
        att[rows,:]=acc[...].astype(B)
        return 0
    lax.fori_loop(0,4,tile,0)
    wocp.wait()
    def outp(i,_):
        lc=pl.multiple_of(i*256,256)
        for dst,off in ((send_ref,ooff),(keep_ref,hoff)):
            col=pl.ds(pl.multiple_of(off+lc,256),256)
            for rb in range(2):
                rows=slice(rb*256,rb*256+256)
                dst[rows,pl.ds(lc,256)]=dot(att[rows,:],wo[:,col]).astype(B)
        return 0
    lax.fori_loop(0,4,outp,0)

def layer(lens,age,order,head,own,oth,cos,sin,w3,wo,kv):
    vm=pl.BlockSpec(memory_space=pltpu.VMEM); an=pl.BlockSpec(memory_space=pl.ANY); sm=pl.BlockSpec(memory_space=pltpu.SMEM)
    return pl.pallas_call(layer_body,
        out_shape=(jax.ShapeDtypeStruct((512,1024),B),)*2,
        in_specs=[sm]*4+[vm]*4+[an]*3, out_specs=(vm,vm),
        scratch_shapes=[pltpu.VMEM((3,2048,1024),B),pltpu.VMEM((1024,2048),B),pltpu.VMEM((1536,1024),B),pltpu.VMEM((1536,1024),B),
            pltpu.VMEM((512,2048),B),pltpu.VMEM((512,1024),B),pltpu.VMEM((512,1024),B),pltpu.VMEM((512,1024),B),pltpu.VMEM((512,1024),B),
            pltpu.VMEM((8,128,768),F),pltpu.VMEM((8,128,384),B),pltpu.VMEM((128,1024),F),
            pltpu.SemaphoreType.DMA((3,)),pltpu.SemaphoreType.DMA,pltpu.SemaphoreType.DMA((24,))],
        compiler_params=pltpu.CompilerParams(vmem_limit_bytes=60<<20),
        cost_estimate=pl.CostEstimate(flops=14*10**9,bytes_accessed=26<<20,transcendentals=4<<20),
        name='layer')(lens,age,order,head,own,oth,cos,sin,w3,wo,kv)

def tables(lens,age):
    ends=jnp.cumsum(lens); starts=ends-lens
    t=jnp.arange(512,dtype=jnp.int32)
    mem=((t[:,None]>=starts[None,:])&(t[:,None]<ends[None,:])).astype(jnp.int32)
    pos=t+jnp.sum(mem*(age-starts)[None,:],axis=1)
    j=jnp.arange(128,dtype=jnp.int32)
    freq=10000.0**(-2.0*(j%64).astype(F)/128)
    ang=pos.astype(F)[:,None]*freq[None,:]
    return jnp.cos(ang), jnp.where(j[None,:]<64,-1.0,1.0)*jnp.sin(ang)

def rows_view(x):
    return x.reshape(512,4,8,128).transpose(0,2,1,3).reshape(16384,128)

def rows_unview(x):
    return x.reshape(512,8,4,128).transpose(0,2,1,3).reshape(512,4,1024)

NCH=8
TCH=512//NCH

def mix_body(r_ref,x_hbm,o_ref,x,sem):
    cps=[pltpu.make_async_copy(x_hbm.at[pl.ds(c*TCH*32,TCH*32),:],x.at[pl.ds(c*TCH*32,TCH*32),:],sem.at[c]) for c in range(NCH)]
    for c in cps: c.start()
    sh=(64,256); row=io(sh,0); col=io(sh,1)
    c=col&3
    a=jnp.where(c==0,r_ref[0],jnp.where(c==1,r_ref[1],jnp.where(c==2,r_ref[2],r_ref[3])))
    a=jnp.where(((col>>5)==(row&7))&(((col>>2)&7)==(row>>3)),a,0.0)
    hi=a.astype(B)
    A=jnp.concatenate([hi,(a-hi.astype(F)).astype(B)],axis=0)
    for ch in range(NCH):
        cps[ch].wait()
        for g in range(ch*TCH//16,(ch+1)*TCH//16):
            X=jnp.concatenate([x[g*512:g*512+256,:],x[g*512+256:g*512+512,:]],axis=1)
            o=dot(A,X)
            o=o[0:64]+o[64:128]
            for j in range(8):
                o_ref[g*16:g*16+16,j*128:(j+1)*128]=jnp.concatenate([o[j*8:j*8+8,0:128],o[j*8:j*8+8,128:256]],axis=0).astype(B)

def mix(x,r):
    return pl.pallas_call(mix_body,out_shape=jax.ShapeDtypeStruct((512,1024),B),
      in_specs=[pl.BlockSpec(memory_space=pltpu.SMEM),pl.BlockSpec(memory_space=pl.ANY)],
      out_specs=pl.BlockSpec(memory_space=pltpu.VMEM),
      scratch_shapes=[pltpu.VMEM((16384,128),B),pltpu.SemaphoreType.DMA((NCH,))],
      compiler_params=pltpu.CompilerParams(vmem_limit_bytes=60<<20),
      cost_estimate=pl.CostEstimate(flops=10**8,bytes_accessed=6<<20,transcendentals=0),
      name='mix')(r,x)

def fin_body(c_ref,w_ref,x_hbm,a_ref,b_ref,o_hbm,x,o,m_ref,wm_ref,isem,osem):
    icp=[pltpu.make_async_copy(x_hbm.at[pl.ds(c*TCH*32,TCH*32),:],x.at[pl.ds(c*TCH*32,TCH*32),:],isem.at[c]) for c in range(NCH)]
    ocp=[pltpu.make_async_copy(o.at[pl.ds(c*TCH*32,TCH*32),:],o_hbm.at[pl.ds(c*TCH*32,TCH*32),:],osem.at[c]) for c in range(NCH)]
    for c in icp: c.start()
    n=128
    row=io((n,n),0); col=io((n,n),1)
    a=jnp.zeros((n,n),F)
    for i in range(4):
        for j in range(4):
            a=jnp.where(((row&3)==j)&((col&3)==i),c_ref[i*4+j],a)
    a=jnp.where((row>>2)==(col>>2),a,0.0)
    hi=a.astype(B); m_ref[:,0:n]=hi; m_ref[:,n:2*n]=(a-hi.astype(F)).astype(B)
    for s in range(2):
        row=io((n,64),0); col=io((n,64),1)
        a=jnp.zeros((n,64),F)
        for j in range(4): a=jnp.where((row&3)==j,w_ref[j],a)
        a=jnp.where(((row>>5)+s*4==(col&7))&(((row>>2)&7)==(col>>3)),a,0.0)
        hi=a.astype(B); lo=(a-hi.astype(F)).astype(B)
        wm_ref[s*n:(s+1)*n,:]=jnp.concatenate([hi,lo,hi,lo],axis=1)
    M=m_ref[...]
    for ch in range(NCH):
        icp[ch].wait()
        for g in range(ch*TCH//16,(ch+1)*TCH//16):
            def U(ref):
                u=ref[g*16:g*16+16,:].astype(F)
                return jnp.concatenate([jnp.concatenate([u[0:8,j*128:(j+1)*128],u[8:16,j*128:(j+1)*128]],axis=1) for j in range(8)],axis=0).astype(B)
            Ua=U(a_ref);Ub=U(b_ref)
            ou=dot(wm_ref[...],jnp.concatenate([Ua,Ua,Ub,Ub],axis=0))
            r0=g*512
            for s in range(2):
                X=jnp.concatenate([x[r0+s*128:r0+s*128+128,:],x[r0+256+s*128:r0+256+s*128+128,:]],axis=1)
                z=(dot(M,jnp.concatenate([X,X],axis=0))+ou[s*128:(s+1)*128]).astype(B)
                o[r0+s*128:r0+s*128+128,:]=z[:,0:128]; o[r0+256+s*128:r0+256+s*128+128,:]=z[:,128:256]
        ocp[ch].start()
    for c in ocp: c.wait()

def fin(x,u1,u2,cr,w):
    vm=pl.BlockSpec(memory_space=pltpu.VMEM); an=pl.BlockSpec(memory_space=pl.ANY); sm=pl.BlockSpec(memory_space=pltpu.SMEM)
    return pl.pallas_call(fin_body,out_shape=jax.ShapeDtypeStruct((16384,128),B),
      in_specs=[sm,sm,an,vm,vm],out_specs=an,
      scratch_shapes=[pltpu.VMEM((16384,128),B),pltpu.VMEM((16384,128),B),pltpu.VMEM((128,256),B),pltpu.VMEM((256,256),B),
        pltpu.SemaphoreType.DMA((NCH,)),pltpu.SemaphoreType.DMA((NCH,))],
      compiler_params=pltpu.CompilerParams(vmem_limit_bytes=60<<20),
      cost_estimate=pl.CostEstimate(flops=10**9,bytes_accessed=10<<20,transcendentals=0),
      name='fin')(cr,w,x,u1,u2)

def pick_body(tab_ref,me_ref,src,o1,o2,o3,buf,isem,osem):
    me=me_ref[0]
    icp=[pltpu.make_async_copy(src.at[b],buf.at[b],isem.at[b]) for b in range(4)]
    for c in icp: c.start()
    for c in icp: c.wait()
    cps=[]
    for d,dst in ((1,o1),(2,o2),(3,o3)):
        cnt=jnp.int32(0); first=jnp.int32(0); second=jnp.int32(0)
        for b in range(4):
            hit=(((tab_ref[b]>>3)-me)&63)==d
            first=jnp.where(hit&(cnt==0),b,first)
            second=jnp.where(hit&(cnt==1),b,second)
            cnt=cnt+hit.astype(jnp.int32)
        for s,i in ((0,first),(1,second)):
            c=pltpu.make_async_copy(buf.at[i],dst.at[s],osem.at[2*(d-1)+s]); c.start(); cps.append(c)
    for c in cps: c.wait()

def pick(tab,me,pre):
    an=pl.BlockSpec(memory_space=pl.ANY); sm=pl.BlockSpec(memory_space=pltpu.SMEM)
    return pl.pallas_call(pick_body,out_shape=(jax.ShapeDtypeStruct((2,2,128,1024),B),)*3,
      in_specs=[sm,sm,an],out_specs=(an,)*3,scratch_shapes=[pltpu.VMEM((4,2,128,1024),B),pltpu.SemaphoreType.DMA((4,)),pltpu.SemaphoreType.DMA((6,))],
      compiler_params=pltpu.CompilerParams(vmem_limit_bytes=60<<20),
      cost_estimate=pl.CostEstimate(flops=0,bytes_accessed=6<<20,transcendentals=0),
      name='pick')(tab,me,pre)

def place_body(t0,t1,t2,t3,me_ref,src,r1,r2,r3,out,buf,zero,isem,osem):
    me=me_ref[0]
    used=jnp.int32(0)
    for tab,ref,own in ((t0,src,True),(t1,r1,False),(t2,r2,False),(t3,r3,False)):
        cnt=jnp.int32(0)
        for b in range(4):
            v=tab[b]
            hit=(v>>3)==me
            slot=v&7
            i=b if own else jnp.minimum(cnt,1)
            @pl.when(hit)
            def _(ref=ref,i=i,slot=slot):
                pltpu.make_async_copy(ref.at[i],buf.at[slot],isem.at[slot]).start()
            cnt=cnt+hit.astype(jnp.int32)
            used=used|jnp.where(hit,jnp.int32(1)<<slot,0)
    zero[...]=jnp.zeros_like(zero)
    for s in range(8):
        @pl.when(((used>>s)&1)==0)
        def _(s=s):
            pltpu.make_async_copy(zero,out.at[s],osem.at[s]).start()
    for s in range(8):
        @pl.when(((used>>s)&1)==1)
        def _(s=s):
            pltpu.make_async_copy(src.at[0],buf.at[s],isem.at[s]).wait()
            pltpu.make_async_copy(buf.at[s],out.at[s],osem.at[s]).start()
    for s in range(8):
        pltpu.make_async_copy(zero,out.at[s],osem.at[s]).wait()

def place(tabs,me,pre,r1,r2,r3):
    an=pl.BlockSpec(memory_space=pl.ANY); sm=pl.BlockSpec(memory_space=pltpu.SMEM)
    return pl.pallas_call(place_body,out_shape=jax.ShapeDtypeStruct((8,2,128,1024),B),
      in_specs=[sm]*5+[an]*4,out_specs=an,
      scratch_shapes=[pltpu.VMEM((8,2,128,1024),B),pltpu.VMEM((2,128,1024),B),pltpu.SemaphoreType.DMA((8,)),pltpu.SemaphoreType.DMA((8,))],
      compiler_params=pltpu.CompilerParams(vmem_limit_bytes=60<<20),
      cost_estimate=pl.CostEstimate(flops=0,bytes_accessed=8<<20,transcendentals=0),
      name='place')(*tabs,me,pre,r1,r2,r3)

def ahead(value,steps):
    return lax.ppermute(value,"page",[(s,(s+steps)%64) for s in range(64)])

def swap(value):
    return lax.ppermute(value,"head",[(0,1),(1,0)])

def body(streams,hc_read,hc_carry,hc_write,w_qkv,w_out,req_lengths,req_age,cache_order,cache_kv,prefill_kv,page_table):
    head=lax.axis_index("head").astype(jnp.int32).reshape(1)
    me=lax.axis_index("page").astype(jnp.int32).reshape(1)
    lens=req_lengths[0]; age=req_age[0]; order=cache_order[0]
    x=rows_view(streams)
    own=mix(x,hc_read)
    oth=swap(own)
    pre=prefill_kv.reshape(4,2,128,1024)
    table=page_table
    own_dep,table_dep=lax.optimization_barrier((own,table))
    s1,s2,s3=pick(table_dep,me,pre)
    r1=ahead(s1,1); r2=ahead(s2,2); r3=ahead(s3,3)
    tabs=(table,ahead(table,1),ahead(table,2),ahead(table,3))
    cos,sin=tables(lens,age)
    oth,tabs=lax.optimization_barrier((oth,tabs))
    w3=w_qkv.transpose(1,0,2)
    keep,send=layer(lens,age,order,head,own,oth,cos,sin,w3,w_out,cache_kv)
    recv=swap(send)
    pages=place(tabs,me,pre,r1,r2,r3)
    carry=(jnp.eye(4,dtype=F)+hc_carry).reshape(16)
    new=fin(x,keep,recv,carry,hc_write)
    return rows_unview(new),pages.reshape(8,1,2,128,1024)

def solution(mesh):
    placed=(P("page",None,"head"),P(),P(),P(),P(None,None,"head"),P("head",None),P("page",None),P("page",None),P("page",None),
        P("page",None,None,"head"),P("page",None,None,None,"head"),P("page"))
    return jax.shard_map(body,mesh=mesh,in_specs=placed,out_specs=(P("page",None,"head"),P("page",None,None,None,"head")),check_vma=False)
```

```python
import math

import jax
import jax.numpy as jnp
from jax import lax
from jax.experimental import pallas as pl
from jax.experimental.pallas import tpu as pltpu
from jax.sharding import PartitionSpec as P

F=jnp.float32; B=jnp.bfloat16
NEG=-1e30
def io(shape,d): return lax.broadcasted_iota(jnp.int32,shape,d)
def dot_t(a,b): return lax.dot_general(a,b,(((1,),(1,)),((),())),preferred_element_type=F)
def dot(a,b): return jnp.dot(a,b,preferred_element_type=F)
QSCALE=math.log2(math.e)/math.sqrt(128.0)

def layer_body(len_ref,age_ref,order_ref,head_ref,own_ref,oth_ref,cos_ref,sin_ref,w_hbm,wo_hbm,kv_hbm,keep_ref,send_ref,
               w,wo,kc,vc,nrm,q,k,v,att,s_ref,p_ref,acc,wsem,wosem,csem):
    h=head_ref[0]
    wcp=[pltpu.make_async_copy(w_hbm.at[c],w.at[c],wsem.at[c]) for c in range(3)]
    for c in wcp: c.start()
    ccp=[]
    for i in range(12):
        pg=order_ref[i]
        ccp.append(pltpu.make_async_copy(kv_hbm.at[pg,0],kc.at[pl.ds(i*128,128),:],csem.at[2*i]))
        ccp.append(pltpu.make_async_copy(kv_hbm.at[pg,1],vc.at[pl.ds(i*128,128),:],csem.at[2*i+1]))
    for c in ccp: c.start()
    wocp=pltpu.make_async_copy(wo_hbm,wo,wosem)
    wocp.start()
    hoff=pl.multiple_of(h*1024,1024); ooff=pl.multiple_of((1-h)*1024,1024)
    def ln(i,_):
        r=pl.ds(pl.multiple_of(i*64,64),64)
        a=own_ref[r,:].astype(F); b=oth_ref[r,:].astype(F)
        m=(jnp.sum(a,axis=1,keepdims=True)+jnp.sum(b,axis=1,keepdims=True))*(1.0/2048)
        a=a-m; b=b-m
        var=(jnp.sum(a*a,axis=1,keepdims=True)+jnp.sum(b*b,axis=1,keepdims=True))*(1.0/2048)
        rs=lax.rsqrt(var+1e-5)
        nrm[r,pl.ds(hoff,1024)]=(a*rs).astype(B)
        nrm[r,pl.ds(ooff,1024)]=(b*rs).astype(B)
        return 0
    lax.fori_loop(0,8,ln,0)
    for c,dst in ((0,q),(1,k),(2,v)):
        wcp[c].wait()
        def proj(i,_,c=c,dst=dst):
            col=pl.ds(pl.multiple_of(i*256,256),256)
            for rb in range(2):
                rows=slice(rb*256,rb*256+256)
                x=dot(nrm[rows,:],w[c,:,col])
                if c<2:
                    co=cos_ref[rows,:]; si=sin_ref[rows,:]
                    y=[]
                    for hh in range(2):
                        xh=x[:,hh*128:hh*128+128]
                        z=xh*co+pltpu.roll(xh,64,1)*si
                        if c==0: z=z*QSCALE
                        y.append(z)
                    x=jnp.concatenate(y,axis=1)
                dst[rows,col]=x.astype(B)
            return 0
        lax.fori_loop(0,4,proj,0)
    for c in ccp: c.wait()
    e=[len_ref[0],len_ref[0]+len_ref[1],len_ref[0]+len_ref[1]+len_ref[2]]
    def tile(t,_):
        t0=t*128
        rows=pl.ds(pl.multiple_of(t0,128),128)
        kb=jnp.maximum(t-2,0)*128
        win=pl.ds(pl.multiple_of(kb,128),384)
        ri=t0+io((128,384),0); ki=kb+io((128,384),1)
        st=jnp.where(ri>=e[2],e[2],jnp.where(ri>=e[1],e[1],jnp.where(ri>=e[0],e[0],0)))
        bias=jnp.where((ki>=st)&(ki<=ri),0.0,NEG)
        for hh in range(8):
            hs=slice(hh*128,hh*128+128)
            s_ref[hh,:,384:768]=dot_t(q[rows,hs],k[win,hs])+bias
        rid=t0+io((128,1),0)
        rreq=(rid>=e[0]).astype(jnp.int32)+(rid>=e[1]).astype(jnp.int32)+(rid>=e[2]).astype(jnp.int32)
        last=t0+127
        lo=(t0>=e[0]).astype(jnp.int32)+(t0>=e[1]).astype(jnp.int32)+(t0>=e[2]).astype(jnp.int32)
        hi=(last>=e[0]).astype(jnp.int32)+(last>=e[1]).astype(jnp.int32)+(last>=e[2]).astype(jnp.int32)
        def sc(r,_):
            cb=jnp.where(io((1,384),1)<age_ref[r],0.0,NEG)
            keys=pl.ds(pl.multiple_of(r*384,384),384)
            mine=rreq==r
            for hh in range(8):
                hs=slice(hh*128,hh*128+128)
                x=dot_t(q[rows,hs],kc[keys,hs])+cb
                s_ref[hh,:,0:384]=jnp.where(mine,x,s_ref[hh,:,0:384])
            return 0
        lax.fori_loop(lo,hi+1,sc,0)
        for hh in range(8):
            hs=slice(hh*128,hh*128+128)
            s=s_ref[hh]
            m=jnp.max(s,axis=1,keepdims=True)
            p=jnp.exp2(s-m)
            l=jnp.sum(p,axis=1,keepdims=True)
            p=(p*(1.0/l)).astype(B)
            p_ref[hh]=p[:,0:384]
            acc[:,hs]=dot(p[:,384:768],v[win,hs])
        def pv(r,_):
            keys=pl.ds(pl.multiple_of(r*384,384),384)
            mine=rreq==r
            for hh in range(8):
                hs=slice(hh*128,hh*128+128)
                pm=jnp.where(mine,p_ref[hh],jnp.zeros((),B))
                acc[:,hs]=acc[:,hs]+dot(pm,vc[keys,hs])
            return 0
        lax.fori_loop(lo,hi+1,pv,0)
        att[rows,:]=acc[...].astype(B)
        return 0
    lax.fori_loop(0,4,tile,0)
    wocp.wait()
    def outp(i,_):
        lc=pl.multiple_of(i*256,256)
        for dst,off in ((send_ref,ooff),(keep_ref,hoff)):
            col=pl.ds(pl.multiple_of(off+lc,256),256)
            for rb in range(2):
                rows=slice(rb*256,rb*256+256)
                dst[rows,pl.ds(lc,256)]=dot(att[rows,:],wo[:,col]).astype(B)
        return 0
    lax.fori_loop(0,4,outp,0)

def layer(lens,age,order,head,own,oth,cos,sin,w3,wo,kv):
    vm=pl.BlockSpec(memory_space=pltpu.VMEM); an=pl.BlockSpec(memory_space=pl.ANY); sm=pl.BlockSpec(memory_space=pltpu.SMEM)
    return pl.pallas_call(layer_body,
        out_shape=(jax.ShapeDtypeStruct((512,1024),B),)*2,
        in_specs=[sm]*4+[vm]*4+[an]*3, out_specs=(vm,vm),
        scratch_shapes=[pltpu.VMEM((3,2048,1024),B),pltpu.VMEM((1024,2048),B),pltpu.VMEM((1536,1024),B),pltpu.VMEM((1536,1024),B),
            pltpu.VMEM((512,2048),B),pltpu.VMEM((512,1024),B),pltpu.VMEM((512,1024),B),pltpu.VMEM((512,1024),B),pltpu.VMEM((512,1024),B),
            pltpu.VMEM((8,128,768),F),pltpu.VMEM((8,128,384),B),pltpu.VMEM((128,1024),F),
            pltpu.SemaphoreType.DMA((3,)),pltpu.SemaphoreType.DMA,pltpu.SemaphoreType.DMA((24,))],
        compiler_params=pltpu.CompilerParams(vmem_limit_bytes=48<<20),
        cost_estimate=pl.CostEstimate(flops=14*10**9,bytes_accessed=26<<20,transcendentals=4<<20),
        name='layer')(lens,age,order,head,own,oth,cos,sin,w3,wo,kv)

def tables(lens,age):
    ends=jnp.cumsum(lens); starts=ends-lens
    t=jnp.arange(512,dtype=jnp.int32)
    mem=((t[:,None]>=starts[None,:])&(t[:,None]<ends[None,:])).astype(jnp.int32)
    pos=t+jnp.sum(mem*(age-starts)[None,:],axis=1)
    j=jnp.arange(128,dtype=jnp.int32)
    freq=10000.0**(-2.0*(j%64).astype(F)/128)
    ang=pos.astype(F)[:,None]*freq[None,:]
    return jnp.cos(ang), jnp.where(j[None,:]<64,-1.0,1.0)*jnp.sin(ang)

def rows_view(x):
    return x.reshape(512,4,8,128).transpose(0,2,1,3).reshape(16384,128)

def rows_unview(x):
    return x.reshape(512,8,4,128).transpose(0,2,1,3).reshape(512,4,1024)

NCH=8
TCH=512//NCH

def mix_body(r_ref,x_hbm,o_ref,x,sem):
    cps=[pltpu.make_async_copy(x_hbm.at[pl.ds(c*TCH*32,TCH*32),:],x.at[pl.ds(c*TCH*32,TCH*32),:],sem.at[c]) for c in range(NCH)]
    for c in cps: c.start()
    sh=(64,256); row=io(sh,0); col=io(sh,1)
    c=col&3
    a=jnp.where(c==0,r_ref[0],jnp.where(c==1,r_ref[1],jnp.where(c==2,r_ref[2],r_ref[3])))
    a=jnp.where(((col>>5)==(row&7))&(((col>>2)&7)==(row>>3)),a,0.0)
    hi=a.astype(B)
    A=jnp.concatenate([hi,(a-hi.astype(F)).astype(B)],axis=0)
    for ch in range(NCH):
        cps[ch].wait()
        for g in range(ch*TCH//16,(ch+1)*TCH//16):
            X=jnp.concatenate([x[g*512:g*512+256,:],x[g*512+256:g*512+512,:]],axis=1)
            o=dot(A,X)
            o=o[0:64]+o[64:128]
            for j in range(8):
                o_ref[g*16:g*16+16,j*128:(j+1)*128]=jnp.concatenate([o[j*8:j*8+8,0:128],o[j*8:j*8+8,128:256]],axis=0).astype(B)

def mix(x,r):
    return pl.pallas_call(mix_body,out_shape=jax.ShapeDtypeStruct((512,1024),B),
      in_specs=[pl.BlockSpec(memory_space=pltpu.SMEM),pl.BlockSpec(memory_space=pl.ANY)],
      out_specs=pl.BlockSpec(memory_space=pltpu.VMEM),
      scratch_shapes=[pltpu.VMEM((16384,128),B),pltpu.SemaphoreType.DMA((NCH,))],
      compiler_params=pltpu.CompilerParams(vmem_limit_bytes=61<<20),
      cost_estimate=pl.CostEstimate(flops=10**8,bytes_accessed=6<<20,transcendentals=0),
      name='mix')(r,x)

def fin_body(c_ref,w_ref,x_hbm,a_ref,b_ref,o_hbm,x,o,m_ref,wm_ref,isem,osem):
    icp=[pltpu.make_async_copy(x_hbm.at[pl.ds(c*TCH*32,TCH*32),:],x.at[pl.ds(c*TCH*32,TCH*32),:],isem.at[c]) for c in range(NCH)]
    ocp=[pltpu.make_async_copy(o.at[pl.ds(c*TCH*32,TCH*32),:],o_hbm.at[pl.ds(c*TCH*32,TCH*32),:],osem.at[c]) for c in range(NCH)]
    for c in icp: c.start()
    n=128
    row=io((n,n),0); col=io((n,n),1)
    a=jnp.zeros((n,n),F)
    for i in range(4):
        for j in range(4):
            a=jnp.where(((row&3)==j)&((col&3)==i),c_ref[i*4+j],a)
    a=jnp.where((row>>2)==(col>>2),a,0.0)
    hi=a.astype(B); m_ref[:,0:n]=hi; m_ref[:,n:2*n]=(a-hi.astype(F)).astype(B)
    for s in range(2):
        row=io((n,64),0); col=io((n,64),1)
        a=jnp.zeros((n,64),F)
        for j in range(4): a=jnp.where((row&3)==j,w_ref[j],a)
        a=jnp.where(((row>>5)+s*4==(col&7))&(((row>>2)&7)==(col>>3)),a,0.0)
        hi=a.astype(B); lo=(a-hi.astype(F)).astype(B)
        wm_ref[s*n:(s+1)*n,:]=jnp.concatenate([hi,lo,hi,lo],axis=1)
    M=m_ref[...]
    for ch in range(NCH):
        icp[ch].wait()
        for g in range(ch*TCH//16,(ch+1)*TCH//16):
            def U(ref):
                u=ref[g*16:g*16+16,:].astype(F)
                return jnp.concatenate([jnp.concatenate([u[0:8,j*128:(j+1)*128],u[8:16,j*128:(j+1)*128]],axis=1) for j in range(8)],axis=0).astype(B)
            Ua=U(a_ref);Ub=U(b_ref)
            ou=dot(wm_ref[...],jnp.concatenate([Ua,Ua,Ub,Ub],axis=0))
            r0=g*512
            for s in range(2):
                X=jnp.concatenate([x[r0+s*128:r0+s*128+128,:],x[r0+256+s*128:r0+256+s*128+128,:]],axis=1)
                z=(dot(M,jnp.concatenate([X,X],axis=0))+ou[s*128:(s+1)*128]).astype(B)
                o[r0+s*128:r0+s*128+128,:]=z[:,0:128]; o[r0+256+s*128:r0+256+s*128+128,:]=z[:,128:256]
        ocp[ch].start()
    for c in ocp: c.wait()

def fin(x,u1,u2,cr,w):
    vm=pl.BlockSpec(memory_space=pltpu.VMEM); an=pl.BlockSpec(memory_space=pl.ANY); sm=pl.BlockSpec(memory_space=pltpu.SMEM)
    return pl.pallas_call(fin_body,out_shape=jax.ShapeDtypeStruct((16384,128),B),
      in_specs=[sm,sm,an,vm,vm],out_specs=an,
      scratch_shapes=[pltpu.VMEM((16384,128),B),pltpu.VMEM((16384,128),B),pltpu.VMEM((128,256),B),pltpu.VMEM((256,256),B),
        pltpu.SemaphoreType.DMA((NCH,)),pltpu.SemaphoreType.DMA((NCH,))],
      compiler_params=pltpu.CompilerParams(vmem_limit_bytes=61<<20),
      cost_estimate=pl.CostEstimate(flops=10**9,bytes_accessed=10<<20,transcendentals=0),
      name='fin')(cr,w,x,u1,u2)

PAY=528

def pick_body(tab_ref,me_ref,src,o1,o2,o3,buf,lab,isem,osem):
    me=me_ref[0]
    icp=[pltpu.make_async_copy(src.at[pl.ds(b*256,256),:],buf.at[b],isem.at[b]) for b in range(4)]
    for c in icp: c.start()
    plan=[]
    for d,dst in ((3,o3),(2,o2),(1,o1)):
        cnt=jnp.int32(0); i=[jnp.int32(0)]*2; l=[jnp.int32(-1)]*2
        for b in range(4):
            hit=(((tab_ref[b]>>3)-me)&63)==d
            for s in range(2):
                i[s]=jnp.where(hit&(cnt==s),b,i[s])
                l[s]=jnp.where(hit&(cnt==s),tab_ref[b]&7,l[s])
            cnt=cnt+hit.astype(jnp.int32)
        lab[d-1]=jnp.where(io((16,1024),0)<8,l[0].astype(F),l[1].astype(F)).astype(B)
        plan.append((d,dst,i))
    for c in icp: c.wait()
    cps=[]
    for d,dst,i in plan:
        for s in range(2):
            cps.append(pltpu.make_async_copy(buf.at[i[s]],dst.at[pl.ds(s*256,256),:],osem.at[3*(d-1)+s]))
        cps.append(pltpu.make_async_copy(lab.at[d-1],dst.at[pl.ds(512,16),:],osem.at[3*(d-1)+2]))
    for c in cps: c.start()
    for c in cps: c.wait()

def pick(tab,me,pre):
    an=pl.BlockSpec(memory_space=pl.ANY); sm=pl.BlockSpec(memory_space=pltpu.SMEM)
    return pl.pallas_call(pick_body,out_shape=(jax.ShapeDtypeStruct((PAY,1024),B),)*3,
      in_specs=[sm,sm,an],out_specs=(an,)*3,
      scratch_shapes=[pltpu.VMEM((4,256,1024),B),pltpu.VMEM((3,16,1024),B),pltpu.SemaphoreType.DMA((4,)),pltpu.SemaphoreType.DMA((9,))],
      compiler_params=pltpu.CompilerParams(vmem_limit_bytes=61<<20),
      cost_estimate=pl.CostEstimate(flops=0,bytes_accessed=6<<20,transcendentals=0),
      name='pick')(tab,me,pre)

def place_body(tab,me_ref,src,r1,r2,r3,out,buf,zero,lab,lsem,isem,osem):
    me=me_ref[0]
    used=jnp.int32(0)
    lcp=[pltpu.make_async_copy(r.at[pl.ds(512,16),:],lab.at[d],lsem.at[d]) for d,r in enumerate((r1,r2,r3))]
    for c in lcp: c.start()
    def fetch(hit,ref,start,slot):
        @pl.when(hit)
        def _():
            pltpu.make_async_copy(ref.at[pl.ds(start,256),:],buf.at[slot],isem.at[slot]).start()
    for b in range(4):
        hit=(tab[b]>>3)==me
        slot=tab[b]&7
        fetch(hit,src,b*256,slot)
        used=used|jnp.where(hit,jnp.int32(1)<<slot,0)
    for d,ref in enumerate((r1,r2,r3)):
        lcp[d].wait()
        for s in range(2):
            v=jnp.max(lab[d,:,0:128].astype(F)[s*8:s*8+8]).astype(jnp.int32)
            hit=v>=0
            slot=v&7
            fetch(hit,ref,s*256,slot)
            used=used|jnp.where(hit,jnp.int32(1)<<slot,0)
    zero[...]=jnp.zeros_like(zero)
    for s in range(8):
        @pl.when(((used>>s)&1)==0)
        def _(s=s):
            pltpu.make_async_copy(zero,out.at[s],osem.at[s]).start()
    for s in range(8):
        @pl.when(((used>>s)&1)==1)
        def _(s=s):
            pltpu.make_async_copy(src.at[pl.ds(0,256),:],buf.at[s],isem.at[s]).wait()
            pltpu.make_async_copy(buf.at[s],out.at[s],osem.at[s]).start()
    for s in range(8):
        pltpu.make_async_copy(zero,out.at[s],osem.at[s]).wait()

def place(tab,me,pre,r1,r2,r3):
    an=pl.BlockSpec(memory_space=pl.ANY); sm=pl.BlockSpec(memory_space=pltpu.SMEM)
    return pl.pallas_call(place_body,out_shape=jax.ShapeDtypeStruct((8,256,1024),B),
      in_specs=[sm]*2+[an]*4,out_specs=an,
      scratch_shapes=[pltpu.VMEM((8,256,1024),B),pltpu.VMEM((256,1024),B),pltpu.VMEM((3,16,1024),B),
        pltpu.SemaphoreType.DMA((3,)),pltpu.SemaphoreType.DMA((8,)),pltpu.SemaphoreType.DMA((8,))],
      compiler_params=pltpu.CompilerParams(vmem_limit_bytes=61<<20),
      cost_estimate=pl.CostEstimate(flops=0,bytes_accessed=8<<20,transcendentals=0),
      name='place')(tab,me,pre,r1,r2,r3)

def ahead(value,steps):
    return lax.ppermute(value,"page",[(s,(s+steps)%64) for s in range(64)])

def swap(value):
    return lax.ppermute(value,"head",[(0,1),(1,0)])

def body(streams,hc_read,hc_carry,hc_write,w_qkv,w_out,req_lengths,req_age,cache_order,cache_kv,prefill_kv,page_table):
    head=lax.axis_index("head").astype(jnp.int32).reshape(1)
    me=lax.axis_index("page").astype(jnp.int32).reshape(1)
    lens=req_lengths[0]; age=req_age[0]; order=cache_order[0]
    x=rows_view(streams)
    own=mix(x,hc_read)
    oth=swap(own)
    pre=prefill_kv.reshape(1024,1024)
    own_dep,table=lax.optimization_barrier((own,page_table))
    s1,s2,s3=pick(table,me,pre)
    r3=ahead(s3,3)
    cos,sin=tables(lens,age)
    oth,s1,s2=lax.optimization_barrier((oth,s1,s2))
    r2=ahead(s2,2); r1=ahead(s1,1)
    w3=w_qkv.transpose(1,0,2)
    keep,send=layer(lens,age,order,head,own,oth,cos,sin,w3,w_out,cache_kv)
    recv=swap(send)
    pages=place(page_table,me,pre,r1,r2,r3)
    recv,pages=lax.optimization_barrier((recv,pages))
    carry=(jnp.eye(4,dtype=F)+hc_carry).reshape(16)
    new=fin(x,keep,recv,carry,hc_write)
    return rows_unview(new),pages.reshape(8,1,2,128,1024)

def solution(mesh):
    placed=(P("page",None,"head"),P(),P(),P(),P(None,None,"head"),P("head",None),P("page",None),P("page",None),P("page",None),
        P("page",None,None,"head"),P("page",None,None,None,"head"),P("page"))
    return jax.shard_map(body,mesh=mesh,in_specs=placed,out_specs=(P("page",None,"head"),P("page",None,None,None,"head")),check_vma=False)
```

```python
import functools
import math

import jax
import jax.numpy as jnp
from jax import lax
from jax.experimental import pallas as pl
from jax.experimental.pallas import tpu as pltpu
from jax.sharding import PartitionSpec as P

F=jnp.float32; B=jnp.bfloat16
NEG=-1e30
def io(shape,d): return lax.broadcasted_iota(jnp.int32,shape,d)
def dot_t(a,b): return lax.dot_general(a,b,(((1,),(1,)),((),())),preferred_element_type=F)
def dot(a,b): return jnp.dot(a,b,preferred_element_type=F)
QSCALE=math.log2(math.e)/math.sqrt(128.0)

def proj_body(head_ref,own0,own1,oth0,oth1,cos_ref,sin_ref,wq,wk,wv,q,k,v,nrm):
    h=head_ref[0]
    hoff=pl.multiple_of(h*1024,1024); ooff=pl.multiple_of((1-h)*1024,1024)
    for half,(own_ref,oth_ref) in enumerate(((own0,oth0),(own1,oth1))):
        def ln(i,_,half=half,own_ref=own_ref,oth_ref=oth_ref):
            r=pl.ds(pl.multiple_of(i*16,16),16)
            o=pl.ds(pl.multiple_of(half*256+i*16,16),16)
            a=own_ref[r,:].astype(F); b=oth_ref[r,:].astype(F)
            m=jnp.sum(a+b,axis=1,keepdims=True)*(1.0/2048)
            a=a-m; b=b-m
            var=jnp.sum(a*a+b*b,axis=1,keepdims=True)*(1.0/2048)
            rs=lax.rsqrt(var+1e-5)
            nrm[o,pl.ds(hoff,1024)]=(a*rs).astype(B)
            nrm[o,pl.ds(ooff,1024)]=(b*rs).astype(B)
            return 0
        lax.fori_loop(0,16,ln,0,unroll=8)
    for c,dst,w in ((0,q,wq),(1,k,wk),(2,v,wv)):
        def proj(i,_,c=c,dst=dst,w=w):
            col=pl.ds(pl.multiple_of(i*256,256),256)
            for rb in range(2):
                rows=slice(rb*256,rb*256+256)
                x=dot(nrm[rows,:],w[:,col])
                if c<2:
                    co=cos_ref[rows,:]; si=sin_ref[rows,:]
                    y=[]
                    for hh in range(2):
                        xh=x[:,hh*128:hh*128+128]
                        z=xh*co+pltpu.roll(xh,64,1)*si
                        if c==0: z=z*QSCALE
                        y.append(z)
                    x=jnp.concatenate(y,axis=1)
                dst[rows,col]=x.astype(B)
            return 0
        lax.fori_loop(0,4,proj,0)

def proj(head,own0,own1,oth0,oth1,cos,sin,wq,wk,wv):
    vm=pl.BlockSpec(memory_space=pltpu.VMEM); sm=pl.BlockSpec(memory_space=pltpu.SMEM)
    return pl.pallas_call(proj_body,out_shape=(jax.ShapeDtypeStruct((512,1024),B),)*3,
        in_specs=[sm]+[vm]*9,out_specs=(vm,)*3,scratch_shapes=[pltpu.VMEM((512,2048),B)],
        compiler_params=pltpu.CompilerParams(vmem_limit_bytes=12<<20),
        cost_estimate=pl.CostEstimate(flops=7*10**9,bytes_accessed=16<<20,transcendentals=0),
        name='proj')(head,own0,own1,oth0,oth1,cos,sin,wq,wk,wv)

def attn_body(len_ref,age_ref,head_ref,q,k,v,kc,vc,wo_hbm,*rest):
    keeps=rest[:NF]; sends=rest[NF:2*NF]
    (wo,att,s_ref,p_ref,acc,wosem)=rest[2*NF:]
    wocp=pltpu.make_async_copy(wo_hbm,wo,wosem)
    wocp.start()
    h=head_ref[0]
    hoff=pl.multiple_of(h*1024,1024); ooff=pl.multiple_of((1-h)*1024,1024)
    e=[len_ref[0],len_ref[0]+len_ref[1],len_ref[0]+len_ref[1]+len_ref[2]]
    def tile(t,_):
        t0=t*128
        rows=pl.ds(pl.multiple_of(t0,128),128)
        kb=jnp.maximum(t-2,0)*128
        win=pl.ds(pl.multiple_of(kb,128),384)
        ri=t0+io((128,384),0); ki=kb+io((128,384),1)
        st=jnp.where(ri>=e[2],e[2],jnp.where(ri>=e[1],e[1],jnp.where(ri>=e[0],e[0],0)))
        bias=jnp.where((ki>=st)&(ki<=ri),0.0,NEG)
        for hh in range(8):
            hs=slice(hh*128,hh*128+128)
            s_ref[hh,:,384:768]=dot_t(q[rows,hs],k[win,hs])+bias
        rid=t0+io((128,1),0)
        rreq=(rid>=e[0]).astype(jnp.int32)+(rid>=e[1]).astype(jnp.int32)+(rid>=e[2]).astype(jnp.int32)
        last=t0+127
        lo=(t0>=e[0]).astype(jnp.int32)+(t0>=e[1]).astype(jnp.int32)+(t0>=e[2]).astype(jnp.int32)
        hi=(last>=e[0]).astype(jnp.int32)+(last>=e[1]).astype(jnp.int32)+(last>=e[2]).astype(jnp.int32)
        def sc(r,_):
            cb=jnp.where(io((1,384),1)<age_ref[r],0.0,NEG)
            keys=pl.ds(pl.multiple_of(r*384,384),384)
            mine=rreq==r
            for hh in range(8):
                hs=slice(hh*128,hh*128+128)
                x=dot_t(q[rows,hs],kc[keys,hs])+cb
                s_ref[hh,:,0:384]=jnp.where(mine,x,s_ref[hh,:,0:384])
            return 0
        lax.fori_loop(lo,hi+1,sc,0)
        for hh in range(8):
            hs=slice(hh*128,hh*128+128)
            s=s_ref[hh]
            m=jnp.max(s,axis=1,keepdims=True)
            p=jnp.exp2(s-m)
            l=jnp.sum(p,axis=1,keepdims=True)
            p=(p*(1.0/l)).astype(B)
            p_ref[hh]=p[:,0:384]
            acc[:,hs]=dot(p[:,384:768],v[win,hs])
        def pv(r,_):
            keys=pl.ds(pl.multiple_of(r*384,384),384)
            mine=rreq==r
            for hh in range(8):
                hs=slice(hh*128,hh*128+128)
                pm=jnp.where(mine,p_ref[hh],jnp.zeros((),B))
                acc[:,hs]=acc[:,hs]+dot(pm,vc[keys,hs])
            return 0
        lax.fori_loop(lo,hi+1,pv,0)
        att[rows,:]=acc[...].astype(B)
        return 0
    lax.fori_loop(0,4,tile,0)
    wocp.wait()
    def outp(i,_):
        lc=pl.multiple_of(i*256,256)
        for rb in range(4):
            rows=slice(rb*128,rb*128+128)
            p=max(i for i in range(NF) if CUTS[i]<=rb*128)
            to=slice(rb*128-CUTS[p],rb*128-CUTS[p]+128)
            for dst,off in ((sends[p],ooff),(keeps[p],hoff)):
                dst[to,pl.ds(lc,256)]=dot(att[rows,:],wo[:,pl.ds(pl.multiple_of(off+lc,256),256)]).astype(B)
        return 0
    lax.fori_loop(0,4,outp,0)

def attn(lens,age,head,q,k,v,kc,vc,wo):
    vm=pl.BlockSpec(memory_space=pltpu.VMEM); an=pl.BlockSpec(memory_space=pl.ANY); sm=pl.BlockSpec(memory_space=pltpu.SMEM)
    return pl.pallas_call(attn_body,
        out_shape=tuple(jax.ShapeDtypeStruct((CUTS[i+1]-CUTS[i],1024),B) for i in range(NF))*2,
        in_specs=[sm]*3+[vm]*5+[an], out_specs=(vm,)*(2*NF),
        scratch_shapes=[pltpu.VMEM((1024,2048),B),pltpu.VMEM((512,1024),B),
            pltpu.VMEM((8,128,768),F),pltpu.VMEM((8,128,384),B),pltpu.VMEM((128,1024),F),pltpu.SemaphoreType.DMA],
        compiler_params=pltpu.CompilerParams(vmem_limit_bytes=40<<20),
        cost_estimate=pl.CostEstimate(flops=7*10**9,bytes_accessed=16<<20,transcendentals=4<<20),
        name='attn')(lens,age,head,q,k,v,kc,vc,wo)

def prep_body(order_ref,w_hbm,kv_hbm,wq,wk,wv,kc,vc,wsem,csem):
    cps=[pltpu.make_async_copy(w_hbm.at[c],w,wsem.at[c]) for c,w in enumerate((wq,wk,wv))]
    for i in range(12):
        pg=order_ref[i]
        cps.append(pltpu.make_async_copy(kv_hbm.at[pg,0],kc.at[pl.ds(i*128,128),:],csem.at[2*i]))
        cps.append(pltpu.make_async_copy(kv_hbm.at[pg,1],vc.at[pl.ds(i*128,128),:],csem.at[2*i+1]))
    for c in cps: c.start()
    for c in cps: c.wait()

def prep(order,w3,kv):
    vm=pl.BlockSpec(memory_space=pltpu.VMEM); an=pl.BlockSpec(memory_space=pl.ANY); sm=pl.BlockSpec(memory_space=pltpu.SMEM)
    return pl.pallas_call(prep_body,
        out_shape=tuple(jax.ShapeDtypeStruct(s,B) for s in ((2048,1024),)*3+((1536,1024),)*2),
        in_specs=[sm,an,an],out_specs=(vm,)*5,
        scratch_shapes=[pltpu.SemaphoreType.DMA((3,)),pltpu.SemaphoreType.DMA((24,))],
        compiler_params=pltpu.CompilerParams(vmem_limit_bytes=30<<20),
        cost_estimate=pl.CostEstimate(flops=0,bytes_accessed=46<<20,transcendentals=0),
        name='prep')(order,w3,kv)

def tables(lens,age):
    ends=jnp.cumsum(lens); starts=ends-lens
    t=jnp.arange(512,dtype=jnp.int32)
    mem=((t[:,None]>=starts[None,:])&(t[:,None]<ends[None,:])).astype(jnp.int32)
    pos=t+jnp.sum(mem*(age-starts)[None,:],axis=1)
    j=jnp.arange(128,dtype=jnp.int32)
    freq=10000.0**(-2.0*(j%64).astype(F)/128)
    ang=pos.astype(F)[:,None]*freq[None,:]
    return jnp.cos(ang), jnp.where(j[None,:]<64,-1.0,1.0)*jnp.sin(ang)

def rows_view(x):
    return x.reshape(512,4,8,128).transpose(0,2,1,3).reshape(16384,128)

def rows_unview(x):
    return x.reshape(512,8,4,128).transpose(0,2,1,3).reshape(512,4,1024)

MR=256
NCH=4
TCH=MR//NCH

def mix_body(base,r_ref,x_hbm,o_ref,x,sem):
    cps=[pltpu.make_async_copy(x_hbm.at[pl.ds(base*32+c*TCH*32,TCH*32),:],x.at[pl.ds(c*TCH*32,TCH*32),:],sem.at[c]) for c in range(NCH)]
    for c in cps: c.start()
    sh=(64,256); row=io(sh,0); col=io(sh,1)
    c=col&3
    a=jnp.where(c==0,r_ref[0],jnp.where(c==1,r_ref[1],jnp.where(c==2,r_ref[2],r_ref[3])))
    a=jnp.where(((col>>5)==(row&7))&(((col>>2)&7)==(row>>3)),a,0.0)
    hi=a.astype(B)
    A=jnp.concatenate([hi,(a-hi.astype(F)).astype(B)],axis=0)
    for ch in range(NCH):
        cps[ch].wait()
        for g in range(ch*TCH//16,(ch+1)*TCH//16):
            X=jnp.concatenate([x[g*512:g*512+256,:],x[g*512+256:g*512+512,:]],axis=1)
            o=dot(A,X)
            o=o[0:64]+o[64:128]
            for j in range(8):
                o_ref[g*16:g*16+16,j*128:(j+1)*128]=jnp.concatenate([o[j*8:j*8+8,0:128],o[j*8:j*8+8,128:256]],axis=0).astype(B)

def mix(i,x,r):
    return pl.pallas_call(functools.partial(mix_body,i*MR),out_shape=jax.ShapeDtypeStruct((MR,1024),B),
      in_specs=[pl.BlockSpec(memory_space=pltpu.SMEM),pl.BlockSpec(memory_space=pl.ANY)],
      out_specs=pl.BlockSpec(memory_space=pltpu.VMEM),
      scratch_shapes=[pltpu.VMEM((MR*32,128),B),pltpu.SemaphoreType.DMA((NCH,))],
      compiler_params=pltpu.CompilerParams(vmem_limit_bytes=61<<20),
      cost_estimate=pl.CostEstimate(flops=10**8,bytes_accessed=3<<20,transcendentals=0),
      name='mix')(r,x)

CUTS=(0,384,512)
NF=2
STEP=64

def fin_body(base,size,c_ref,w_ref,x_hbm,a_ref,b_ref,*rest):
    o_hbm,x,o,m_ref,wm_ref,isem,osem=rest[-7:]
    FCH=size//STEP
    def span(c): return pl.ds((base+c*STEP)*32,STEP*32)
    def part(c): return pl.ds(c*STEP*32,STEP*32)
    icp=[pltpu.make_async_copy(x_hbm.at[span(c),:],x.at[part(c),:],isem.at[c]) for c in range(FCH)]
    ocp=[pltpu.make_async_copy(o.at[part(c),:],o_hbm.at[span(c),:],osem.at[c]) for c in range(FCH)]
    for c in icp: c.start()
    n=128
    row=io((n,n),0); col=io((n,n),1)
    a=jnp.zeros((n,n),F)
    for i in range(4):
        for j in range(4):
            a=jnp.where(((row&3)==j)&((col&3)==i),c_ref[i*4+j],a)
    a=jnp.where((row>>2)==(col>>2),a,0.0)
    hi=a.astype(B); m_ref[:,0:n]=hi; m_ref[:,n:2*n]=(a-hi.astype(F)).astype(B)
    for s in range(2):
        row=io((n,64),0); col=io((n,64),1)
        a=jnp.zeros((n,64),F)
        for j in range(4): a=jnp.where((row&3)==j,w_ref[j],a)
        a=jnp.where(((row>>5)+s*4==(col&7))&(((row>>2)&7)==(col>>3)),a,0.0)
        hi=a.astype(B); lo=(a-hi.astype(F)).astype(B)
        wm_ref[s*n:(s+1)*n,:]=jnp.concatenate([hi,lo,hi,lo],axis=1)
    M=m_ref[...]
    for ch in range(FCH):
        icp[ch].wait()
        for g in range(ch*STEP//16,(ch+1)*STEP//16):
            def U(ref):
                u=ref[g*16:g*16+16,:].astype(F)
                return jnp.concatenate([jnp.concatenate([u[0:8,j*128:(j+1)*128],u[8:16,j*128:(j+1)*128]],axis=1) for j in range(8)],axis=0).astype(B)
            Ua=U(a_ref);Ub=U(b_ref)
            ou=dot(wm_ref[...],jnp.concatenate([Ua,Ua,Ub,Ub],axis=0))
            r0=g*512
            for s in range(2):
                X=jnp.concatenate([x[r0+s*128:r0+s*128+128,:],x[r0+256+s*128:r0+256+s*128+128,:]],axis=1)
                z=(dot(M,jnp.concatenate([X,X],axis=0))+ou[s*128:(s+1)*128]).astype(B)
                o[r0+s*128:r0+s*128+128,:]=z[:,0:128]; o[r0+256+s*128:r0+256+s*128+128,:]=z[:,128:256]
        ocp[ch].start()
    for c in ocp: c.wait()

def fin(i,x,u1,u2,cr,w,prev):
    an=pl.BlockSpec(memory_space=pl.ANY); sm=pl.BlockSpec(memory_space=pltpu.SMEM); vm=pl.BlockSpec(memory_space=pltpu.VMEM)
    more=[] if prev is None else [prev]
    base,size=CUTS[i],CUTS[i+1]-CUTS[i]
    return pl.pallas_call(functools.partial(fin_body,base,size),out_shape=jax.ShapeDtypeStruct((16384,128),B),
      in_specs=[sm,sm,an,vm,vm]+[an]*len(more),out_specs=an,
      scratch_shapes=[pltpu.VMEM((size*32,128),B),pltpu.VMEM((size*32,128),B),pltpu.VMEM((128,256),B),pltpu.VMEM((256,256),B),
        pltpu.SemaphoreType.DMA((size//STEP,)),pltpu.SemaphoreType.DMA((size//STEP,))],
      input_output_aliases={5:0} if more else {},
      compiler_params=pltpu.CompilerParams(vmem_limit_bytes=58<<20),
      cost_estimate=pl.CostEstimate(flops=10**9*size//512,bytes_accessed=(10<<20)*size//512,transcendentals=0),
      name='fin')(cr,w,x,u1,u2,*more)

ROWS=2048
PAY=2*ROWS+16

def tiles_view(x):
    n=x.shape[0]
    return x.reshape(n//8,8,8,128).transpose(0,2,1,3).reshape(n*8,128)

def tiles_unview(x):
    n=x.shape[0]//8
    return x.reshape(n//8,8,8,128).transpose(0,2,1,3).reshape(n,1024)

def pick_body(tab_ref,me_ref,src,o1,o2,o3,buf,lab,isem,osem):
    me=me_ref[0]
    icp=[pltpu.make_async_copy(src.at[pl.ds(b*ROWS,ROWS),:],buf.at[b],isem.at[b]) for b in range(4)]
    for c in icp: c.start()
    plan=[]
    for d,dst in ((3,o3),(2,o2),(1,o1)):
        cnt=jnp.int32(0); i=[jnp.int32(0)]*2; l=[jnp.int32(-1)]*2
        for b in range(4):
            hit=(((tab_ref[b]>>3)-me)&63)==d
            for s in range(2):
                i[s]=jnp.where(hit&(cnt==s),b,i[s])
                l[s]=jnp.where(hit&(cnt==s),tab_ref[b]&7,l[s])
            cnt=cnt+hit.astype(jnp.int32)
        lab[d-1]=jnp.where(io((16,128),0)<8,l[0].astype(F),l[1].astype(F)).astype(B)
        plan.append((d,dst,i))
    for c in icp: c.wait()
    cps=[]
    for d,dst,i in plan:
        for s in range(2):
            cps.append(pltpu.make_async_copy(buf.at[i[s]],dst.at[pl.ds(s*ROWS,ROWS),:],osem.at[3*(d-1)+s]))
        cps.append(pltpu.make_async_copy(lab.at[d-1],dst.at[pl.ds(2*ROWS,16),:],osem.at[3*(d-1)+2]))
    for c in cps: c.start()
    for c in cps: c.wait()

def pick(tab,me,pre):
    an=pl.BlockSpec(memory_space=pl.ANY); sm=pl.BlockSpec(memory_space=pltpu.SMEM)
    return pl.pallas_call(pick_body,out_shape=(jax.ShapeDtypeStruct((PAY,128),B),)*3,
      in_specs=[sm,sm,an],out_specs=(an,)*3,
      scratch_shapes=[pltpu.VMEM((4,ROWS,128),B),pltpu.VMEM((3,16,128),B),pltpu.SemaphoreType.DMA((4,)),pltpu.SemaphoreType.DMA((9,))],
      compiler_params=pltpu.CompilerParams(vmem_limit_bytes=12<<20),
      cost_estimate=pl.CostEstimate(flops=0,bytes_accessed=6<<20,transcendentals=0),
      name='pick')(tab,me,pre)

def place_body(tab,me_ref,src,r1,r3,r2,out,buf,zero,isem,osem):
    me=me_ref[0]
    used=jnp.int32(0)
    for b in range(4):
        hit=(tab[b]>>3)==me
        slot=tab[b]&7
        @pl.when(hit)
        def _(b=b,slot=slot):
            pltpu.make_async_copy(src.at[pl.ds(b*ROWS,ROWS),:],buf.at[slot],isem.at[slot]).start()
        used=used|jnp.where(hit,jnp.int32(1)<<slot,0)
    here=used
    for ref,on in ((r1,True),(r3,True),(r2,True)):
        lab=ref[2*ROWS:2*ROWS+16,:].astype(F)
        for s in range(2):
            v=jnp.max(lab[s*8:s*8+8]).astype(jnp.int32)
            hit=(v>=0)&on
            slot=v&7
            @pl.when(hit)
            def _(ref=ref,s=s,slot=slot):
                pltpu.make_async_copy(ref.at[pl.ds(s*ROWS,ROWS),:],out.at[slot],osem.at[slot]).start()
            used=used|jnp.where(hit,jnp.int32(1)<<slot,0)
    zero[...]=jnp.zeros_like(zero)
    for s in range(8):
        @pl.when(((used>>s)&1)==0)
        def _(s=s):
            pltpu.make_async_copy(zero,out.at[s],osem.at[s]).start()
    for s in range(8):
        @pl.when(((here>>s)&1)==1)
        def _(s=s):
            pltpu.make_async_copy(src.at[pl.ds(0,ROWS),:],buf.at[s],isem.at[s]).wait()
            pltpu.make_async_copy(buf.at[s],out.at[s],osem.at[s]).start()
    for s in range(8):
        pltpu.make_async_copy(zero,out.at[s],osem.at[s]).wait()

def place(tab,me,pre,*got):
    an=pl.BlockSpec(memory_space=pl.ANY); sm=pl.BlockSpec(memory_space=pltpu.SMEM); vm=pl.BlockSpec(memory_space=pltpu.VMEM)
    return pl.pallas_call(place_body,out_shape=jax.ShapeDtypeStruct((8,ROWS,128),B),
      in_specs=[sm,sm,an,vm,vm,vm],out_specs=an,
      scratch_shapes=[pltpu.VMEM((8,ROWS,128),B),pltpu.VMEM((ROWS,128),B),
        pltpu.SemaphoreType.DMA((8,)),pltpu.SemaphoreType.DMA((8,))],
      compiler_params=pltpu.CompilerParams(vmem_limit_bytes=12<<20),
      cost_estimate=pl.CostEstimate(flops=0,bytes_accessed=8<<20,transcendentals=0),
      name='place')(tab,me,pre,*got)

def ahead(value,steps):
    return lax.ppermute(value,"page",[(s,(s+steps)%64) for s in range(64)])

def swap(value):
    return lax.ppermute(value,"head",[(0,1),(1,0)])

def body(streams,hc_read,hc_carry,hc_write,w_qkv,w_out,req_lengths,req_age,cache_order,cache_kv,prefill_kv,page_table):
    head=lax.axis_index("head").astype(jnp.int32).reshape(1)
    me=lax.axis_index("page").astype(jnp.int32).reshape(1)
    lens=req_lengths[0]; age=req_age[0]; order=cache_order[0]
    x=rows_view(streams)
    own0=mix(0,x,hc_read)
    oth0=swap(own0)
    x1,own0=lax.optimization_barrier((x,own0))
    own1=mix(1,x1,hc_read)
    oth1=swap(own1)
    pre=tiles_view(prefill_kv.reshape(1024,1024))
    own_dep,table=lax.optimization_barrier((own1,page_table))
    s1,s2,s3=pick(table,me,pre)
    r3=ahead(s3,3); r1=ahead(s1,1)
    cos,sin=tables(lens,age)
    wq,wk,wv,kc,vc=prep(order,w_qkv.transpose(1,0,2),cache_kv)
    oth1,s2,wq,wk,wv,kc,vc=lax.optimization_barrier((oth1,s2,wq,wk,wv,kc,vc))
    r2=ahead(s2,2)
    q,k,v=proj(head,own0,own1,oth0,oth1,cos,sin,wq,wk,wv)
    parts=attn(lens,age,head,q,k,v,kc,vc,w_out)
    keeps,sends=parts[:NF],parts[NF:]
    recvs=[swap(s) for s in sends]
    pages=place(page_table,me,pre,r1,r3,r2)
    carry=(jnp.eye(4,dtype=F)+hc_carry).reshape(16)
    recvs[0],pages=lax.optimization_barrier((recvs[0],pages))
    new=None
    for i in range(NF): new=fin(i,x,keeps[i],recvs[i],carry,hc_write,new)
    return rows_unview(new),tiles_unview(pages.reshape(8*ROWS,128)).reshape(8,1,2,128,1024)

def solution(mesh):
    placed=(P("page",None,"head"),P(),P(),P(),P(None,None,"head"),P("head",None),P("page",None),P("page",None),P("page",None),
        P("page",None,None,"head"),P("page",None,None,None,"head"),P("page"))
    return jax.shard_map(body,mesh=mesh,in_specs=placed,out_specs=(P("page",None,"head"),P("page",None,None,None,"head")),check_vma=False)
```

```python
import functools
import math

import jax
import jax.numpy as jnp
from jax import lax
from jax.experimental import pallas as pl
from jax.experimental.pallas import tpu as pltpu
from jax.sharding import PartitionSpec as P

F=jnp.float32; B=jnp.bfloat16
NEG=-1e30
def io(shape,d): return lax.broadcasted_iota(jnp.int32,shape,d)
def dot_t(a,b): return lax.dot_general(a,b,(((1,),(1,)),((),())),preferred_element_type=F)
def dot(a,b): return jnp.dot(a,b,preferred_element_type=F)
QSCALE=math.log2(math.e)/math.sqrt(128.0)

def proj_body(head_ref,own0,own1,oth0,oth1,cos_ref,sin_ref,wq,wk,wv,q,k,v,nrm):
    h=head_ref[0]
    hoff=pl.multiple_of(h*1024,1024); ooff=pl.multiple_of((1-h)*1024,1024)
    for half,(own_ref,oth_ref) in enumerate(((own0,oth0),(own1,oth1))):
        def ln(i,_,half=half,own_ref=own_ref,oth_ref=oth_ref):
            r=pl.ds(pl.multiple_of(i*16,16),16)
            o=pl.ds(pl.multiple_of(HEADCUT[half]+i*16,16),16)
            a=own_ref[r,:].astype(F); b=oth_ref[r,:].astype(F)
            m=jnp.sum(a+b,axis=1,keepdims=True)*(1.0/2048)
            a=a-m; b=b-m
            var=jnp.sum(a*a+b*b,axis=1,keepdims=True)*(1.0/2048)
            rs=lax.rsqrt(var+1e-5)
            nrm[o,pl.ds(hoff,1024)]=(a*rs).astype(B)
            nrm[o,pl.ds(ooff,1024)]=(b*rs).astype(B)
            return 0
        lax.fori_loop(0,(HEADCUT[half+1]-HEADCUT[half])//16,ln,0,unroll=8)
    for c,dst,w in ((0,q,wq),(1,k,wk),(2,v,wv)):
        def proj(i,_,c=c,dst=dst,w=w):
            col=pl.ds(pl.multiple_of(i*256,256),256)
            for rb in range(2):
                rows=slice(rb*256,rb*256+256)
                x=dot(nrm[rows,:],w[:,col])
                if c<2:
                    co=cos_ref[rows,:]; si=sin_ref[rows,:]
                    y=[]
                    for hh in range(2):
                        xh=x[:,hh*128:hh*128+128]
                        z=xh*co+pltpu.roll(xh,64,1)*si
                        if c==0: z=z*QSCALE
                        y.append(z)
                    x=jnp.concatenate(y,axis=1)
                dst[rows,col]=x.astype(B)
            return 0
        lax.fori_loop(0,4,proj,0)

def proj(head,own0,own1,oth0,oth1,cos,sin,wq,wk,wv):
    vm=pl.BlockSpec(memory_space=pltpu.VMEM); sm=pl.BlockSpec(memory_space=pltpu.SMEM)
    return pl.pallas_call(proj_body,out_shape=(jax.ShapeDtypeStruct((512,1024),B),)*3,
        in_specs=[sm]+[vm]*9,out_specs=(vm,)*3,scratch_shapes=[pltpu.VMEM((512,2048),B)],
        compiler_params=pltpu.CompilerParams(vmem_limit_bytes=12<<20),
        cost_estimate=pl.CostEstimate(flops=7*10**9,bytes_accessed=16<<20,transcendentals=0),
        name='proj')(head,own0,own1,oth0,oth1,cos,sin,wq,wk,wv)

def attn_body(len_ref,age_ref,head_ref,q,k,v,kc,vc,wo_hbm,*rest):
    keeps=rest[:NF]; sends=rest[NF:2*NF]
    (wo,att,s_ref,p_ref,acc,wosem)=rest[2*NF:]
    wocp=pltpu.make_async_copy(wo_hbm,wo,wosem)
    wocp.start()
    h=head_ref[0]
    hoff=pl.multiple_of(h*1024,1024); ooff=pl.multiple_of((1-h)*1024,1024)
    e=[len_ref[0],len_ref[0]+len_ref[1],len_ref[0]+len_ref[1]+len_ref[2]]
    def tile(t,_):
        t0=t*128
        rows=pl.ds(pl.multiple_of(t0,128),128)
        kb=jnp.maximum(t-2,0)*128
        win=pl.ds(pl.multiple_of(kb,128),384)
        ri=t0+io((128,384),0); ki=kb+io((128,384),1)
        st=jnp.where(ri>=e[2],e[2],jnp.where(ri>=e[1],e[1],jnp.where(ri>=e[0],e[0],0)))
        bias=jnp.where((ki>=st)&(ki<=ri),0.0,NEG)
        for hh in range(8):
            hs=slice(hh*128,hh*128+128)
            s_ref[hh,:,384:768]=dot_t(q[rows,hs],k[win,hs])+bias
        rid=t0+io((128,1),0)
        rreq=(rid>=e[0]).astype(jnp.int32)+(rid>=e[1]).astype(jnp.int32)+(rid>=e[2]).astype(jnp.int32)
        last=t0+127
        lo=(t0>=e[0]).astype(jnp.int32)+(t0>=e[1]).astype(jnp.int32)+(t0>=e[2]).astype(jnp.int32)
        hi=(last>=e[0]).astype(jnp.int32)+(last>=e[1]).astype(jnp.int32)+(last>=e[2]).astype(jnp.int32)
        def sc(r,_):
            cb=jnp.where(io((1,384),1)<age_ref[r],0.0,NEG)
            keys=pl.ds(pl.multiple_of(r*384,384),384)
            mine=rreq==r
            for hh in range(8):
                hs=slice(hh*128,hh*128+128)
                x=dot_t(q[rows,hs],kc[keys,hs])+cb
                s_ref[hh,:,0:384]=jnp.where(mine,x,s_ref[hh,:,0:384])
            return 0
        lax.fori_loop(lo,hi+1,sc,0)
        for hh in range(8):
            hs=slice(hh*128,hh*128+128)
            s=s_ref[hh]
            m=jnp.max(s,axis=1,keepdims=True)
            p=jnp.exp2(s-m)
            l=jnp.sum(p,axis=1,keepdims=True)
            p=(p*(1.0/l)).astype(B)
            p_ref[hh]=p[:,0:384]
            acc[:,hs]=dot(p[:,384:768],v[win,hs])
        def pv(r,_):
            keys=pl.ds(pl.multiple_of(r*384,384),384)
            mine=rreq==r
            for hh in range(8):
                hs=slice(hh*128,hh*128+128)
                pm=jnp.where(mine,p_ref[hh],jnp.zeros((),B))
                acc[:,hs]=acc[:,hs]+dot(pm,vc[keys,hs])
            return 0
        lax.fori_loop(lo,hi+1,pv,0)
        att[rows,:]=acc[...].astype(B)
        return 0
    lax.fori_loop(0,4,tile,0)
    wocp.wait()
    def outp(i,_):
        lc=pl.multiple_of(i*256,256)
        for rb in range(4):
            rows=slice(rb*128,rb*128+128)
            p=max(i for i in range(NF) if CUTS[i]<=rb*128)
            to=slice(rb*128-CUTS[p],rb*128-CUTS[p]+128)
            for dst,off in ((sends[p],ooff),(keeps[p],hoff)):
                dst[to,pl.ds(lc,256)]=dot(att[rows,:],wo[:,pl.ds(pl.multiple_of(off+lc,256),256)]).astype(B)
        return 0
    lax.fori_loop(0,4,outp,0)

def attn(lens,age,head,q,k,v,kc,vc,wo):
    vm=pl.BlockSpec(memory_space=pltpu.VMEM); an=pl.BlockSpec(memory_space=pl.ANY); sm=pl.BlockSpec(memory_space=pltpu.SMEM)
    return pl.pallas_call(attn_body,
        out_shape=tuple(jax.ShapeDtypeStruct((CUTS[i+1]-CUTS[i],1024),B) for i in range(NF))*2,
        in_specs=[sm]*3+[vm]*5+[an], out_specs=(vm,)*(2*NF),
        scratch_shapes=[pltpu.VMEM((1024,2048),B),pltpu.VMEM((512,1024),B),
            pltpu.VMEM((8,128,768),F),pltpu.VMEM((8,128,384),B),pltpu.VMEM((128,1024),F),pltpu.SemaphoreType.DMA],
        compiler_params=pltpu.CompilerParams(vmem_limit_bytes=40<<20),
        cost_estimate=pl.CostEstimate(flops=7*10**9,bytes_accessed=16<<20,transcendentals=4<<20),
        name='attn')(lens,age,head,q,k,v,kc,vc,wo)

def prep_body(order_ref,w_hbm,kv_hbm,wq,wk,wv,kc,vc,wsem,csem):
    cps=[pltpu.make_async_copy(w_hbm.at[c],w,wsem.at[c]) for c,w in enumerate((wq,wk,wv))]
    for i in range(12):
        pg=order_ref[i]
        cps.append(pltpu.make_async_copy(kv_hbm.at[pg,0],kc.at[pl.ds(i*128,128),:],csem.at[2*i]))
        cps.append(pltpu.make_async_copy(kv_hbm.at[pg,1],vc.at[pl.ds(i*128,128),:],csem.at[2*i+1]))
    for c in cps: c.start()
    for c in cps: c.wait()

def prep(order,w3,kv):
    vm=pl.BlockSpec(memory_space=pltpu.VMEM); an=pl.BlockSpec(memory_space=pl.ANY); sm=pl.BlockSpec(memory_space=pltpu.SMEM)
    return pl.pallas_call(prep_body,
        out_shape=tuple(jax.ShapeDtypeStruct(s,B) for s in ((2048,1024),)*3+((1536,1024),)*2),
        in_specs=[sm,an,an],out_specs=(vm,)*5,
        scratch_shapes=[pltpu.SemaphoreType.DMA((3,)),pltpu.SemaphoreType.DMA((24,))],
        compiler_params=pltpu.CompilerParams(vmem_limit_bytes=30<<20),
        cost_estimate=pl.CostEstimate(flops=0,bytes_accessed=46<<20,transcendentals=0),
        name='prep')(order,w3,kv)

def tables(lens,age):
    ends=jnp.cumsum(lens); starts=ends-lens
    t=jnp.arange(512,dtype=jnp.int32)
    mem=((t[:,None]>=starts[None,:])&(t[:,None]<ends[None,:])).astype(jnp.int32)
    pos=t+jnp.sum(mem*(age-starts)[None,:],axis=1)
    j=jnp.arange(128,dtype=jnp.int32)
    freq=10000.0**(-2.0*(j%64).astype(F)/128)
    ang=pos.astype(F)[:,None]*freq[None,:]
    return jnp.cos(ang), jnp.where(j[None,:]<64,-1.0,1.0)*jnp.sin(ang)

def rows_view(x):
    return x.reshape(512,4,8,128).transpose(0,2,1,3).reshape(16384,128)

def rows_unview(x):
    return x.reshape(512,8,4,128).transpose(0,2,1,3).reshape(512,4,1024)

HEADCUT=(0,128,512)
TCH=64

def mix_body(base,size,r_ref,x_hbm,o_ref,x,sem):
    NCH=size//TCH
    cps=[pltpu.make_async_copy(x_hbm.at[pl.ds(base*32+c*TCH*32,TCH*32),:],x.at[pl.ds(c*TCH*32,TCH*32),:],sem.at[c]) for c in range(NCH)]
    for c in cps: c.start()
    sh=(64,256); row=io(sh,0); col=io(sh,1)
    c=col&3
    a=jnp.where(c==0,r_ref[0],jnp.where(c==1,r_ref[1],jnp.where(c==2,r_ref[2],r_ref[3])))
    a=jnp.where(((col>>5)==(row&7))&(((col>>2)&7)==(row>>3)),a,0.0)
    hi=a.astype(B)
    A=jnp.concatenate([hi,(a-hi.astype(F)).astype(B)],axis=0)
    for ch in range(NCH):
        cps[ch].wait()
        for g in range(ch*TCH//16,(ch+1)*TCH//16):
            X=jnp.concatenate([x[g*512:g*512+256,:],x[g*512+256:g*512+512,:]],axis=1)
            o=dot(A,X)
            o=o[0:64]+o[64:128]
            for j in range(8):
                o_ref[g*16:g*16+16,j*128:(j+1)*128]=jnp.concatenate([o[j*8:j*8+8,0:128],o[j*8:j*8+8,128:256]],axis=0).astype(B)

def mix(i,x,r):
    base,MR=HEADCUT[i],HEADCUT[i+1]-HEADCUT[i]
    return pl.pallas_call(functools.partial(mix_body,base,MR),out_shape=jax.ShapeDtypeStruct((MR,1024),B),
      in_specs=[pl.BlockSpec(memory_space=pltpu.SMEM),pl.BlockSpec(memory_space=pl.ANY)],
      out_specs=pl.BlockSpec(memory_space=pltpu.VMEM),
      scratch_shapes=[pltpu.VMEM((MR*32,128),B),pltpu.SemaphoreType.DMA((MR//TCH,))],
      compiler_params=pltpu.CompilerParams(vmem_limit_bytes=61<<20),
      cost_estimate=pl.CostEstimate(flops=10**8,bytes_accessed=3<<20,transcendentals=0),
      name='mix')(r,x)

CUTS=(0,384,512)
NF=2
STEP=32

def warm_body(c_ref,w_ref,x_hbm,x,m_ref,wm_ref,sem):
    cp=pltpu.make_async_copy(x_hbm,x,sem)
    cp.start()
    n=128
    row=io((n,n),0); col=io((n,n),1)
    a=jnp.zeros((n,n),F)
    for i in range(4):
        for j in range(4):
            a=jnp.where(((row&3)==j)&((col&3)==i),c_ref[i*4+j],a)
    a=jnp.where((row>>2)==(col>>2),a,0.0)
    hi=a.astype(B); m_ref[:,0:n]=hi; m_ref[:,n:2*n]=(a-hi.astype(F)).astype(B)
    for s in range(2):
        row=io((n,64),0); col=io((n,64),1)
        a=jnp.zeros((n,64),F)
        for j in range(4): a=jnp.where((row&3)==j,w_ref[j],a)
        a=jnp.where(((row>>5)+s*4==(col&7))&(((row>>2)&7)==(col>>3)),a,0.0)
        hi=a.astype(B); lo=(a-hi.astype(F)).astype(B)
        wm_ref[s*n:(s+1)*n,:]=jnp.concatenate([hi,lo,hi,lo],axis=1)
    cp.wait()

def warm(x,cr,w):
    an=pl.BlockSpec(memory_space=pl.ANY); sm=pl.BlockSpec(memory_space=pltpu.SMEM); vm=pl.BlockSpec(memory_space=pltpu.VMEM)
    return pl.pallas_call(warm_body,
      out_shape=(jax.ShapeDtypeStruct((16384,128),B),jax.ShapeDtypeStruct((128,256),B),jax.ShapeDtypeStruct((256,256),B)),
      in_specs=[sm,sm,an],out_specs=(vm,)*3,scratch_shapes=[pltpu.SemaphoreType.DMA],
      compiler_params=pltpu.CompilerParams(vmem_limit_bytes=48<<20),
      cost_estimate=pl.CostEstimate(flops=0,bytes_accessed=8<<20,transcendentals=0),
      name='warm')(cr,w,x)

def fin_body(base,size,x,m_ref,wm_ref,a_ref,b_ref,*rest):
    o_hbm,o,osem=rest[-3:]
    FCH=size//STEP
    ocp=[pltpu.make_async_copy(o.at[pl.ds(c*STEP*32,STEP*32),:],o_hbm.at[pl.ds((base+c*STEP)*32,STEP*32),:],osem.at[c]) for c in range(FCH)]
    M=m_ref[...]
    for ch in range(FCH):
        for g in range(ch*STEP//16,(ch+1)*STEP//16):
            def U(ref):
                u=ref[g*16:g*16+16,:].astype(F)
                return jnp.concatenate([jnp.concatenate([u[0:8,j*128:(j+1)*128],u[8:16,j*128:(j+1)*128]],axis=1) for j in range(8)],axis=0).astype(B)
            Ua=U(a_ref);Ub=U(b_ref)
            ou=dot(wm_ref[...],jnp.concatenate([Ua,Ua,Ub,Ub],axis=0))
            r0=g*512; q0=base*32+r0
            for s in range(2):
                X=jnp.concatenate([x[q0+s*128:q0+s*128+128,:],x[q0+256+s*128:q0+256+s*128+128,:]],axis=1)
                z=(dot(M,jnp.concatenate([X,X],axis=0))+ou[s*128:(s+1)*128]).astype(B)
                o[r0+s*128:r0+s*128+128,:]=z[:,0:128]; o[r0+256+s*128:r0+256+s*128+128,:]=z[:,128:256]
        ocp[ch].start()
    for c in ocp: c.wait()

def fin(i,ready,u1,u2,prev):
    an=pl.BlockSpec(memory_space=pl.ANY); vm=pl.BlockSpec(memory_space=pltpu.VMEM)
    more=[] if prev is None else [prev]
    base,size=CUTS[i],CUTS[i+1]-CUTS[i]
    return pl.pallas_call(functools.partial(fin_body,base,size),out_shape=jax.ShapeDtypeStruct((16384,128),B),
      in_specs=[vm]*5+[an]*len(more),out_specs=an,
      scratch_shapes=[pltpu.VMEM((size*32,128),B),pltpu.SemaphoreType.DMA((size//STEP,))],
      input_output_aliases={5:0} if more else {},
      compiler_params=pltpu.CompilerParams(vmem_limit_bytes=16<<20),
      cost_estimate=pl.CostEstimate(flops=10**9*size//512,bytes_accessed=(10<<20)*size//512,transcendentals=0),
      name='fin')(*ready,u1,u2,*more)

ROWS=2048
PAY=2*ROWS+16

def tiles_view(x):
    n=x.shape[0]
    return x.reshape(n//8,8,8,128).transpose(0,2,1,3).reshape(n*8,128)

def tiles_unview(x):
    n=x.shape[0]//8
    return x.reshape(n//8,8,8,128).transpose(0,2,1,3).reshape(n,1024)

def pick_body(tab_ref,me_ref,src,o1,o2,o3,buf,lab,isem,osem):
    me=me_ref[0]
    icp=[pltpu.make_async_copy(src.at[pl.ds(b*ROWS,ROWS),:],buf.at[b],isem.at[b]) for b in range(4)]
    for c in icp: c.start()
    plan=[]
    for d,dst in ((3,o3),(2,o2),(1,o1)):
        cnt=jnp.int32(0); i=[jnp.int32(0)]*2; l=[jnp.int32(-1)]*2
        for b in range(4):
            hit=(((tab_ref[b]>>3)-me)&63)==d
            for s in range(2):
                i[s]=jnp.where(hit&(cnt==s),b,i[s])
                l[s]=jnp.where(hit&(cnt==s),tab_ref[b]&7,l[s])
            cnt=cnt+hit.astype(jnp.int32)
        lab[d-1]=jnp.where(io((16,128),0)<8,l[0].astype(F),l[1].astype(F)).astype(B)
        plan.append((d,dst,i))
    for c in icp: c.wait()
    cps=[]
    for d,dst,i in plan:
        for s in range(2):
            cps.append(pltpu.make_async_copy(buf.at[i[s]],dst.at[pl.ds(s*ROWS,ROWS),:],osem.at[3*(d-1)+s]))
        cps.append(pltpu.make_async_copy(lab.at[d-1],dst.at[pl.ds(2*ROWS,16),:],osem.at[3*(d-1)+2]))
    for c in cps: c.start()
    for c in cps: c.wait()

def pick(tab,me,pre):
    an=pl.BlockSpec(memory_space=pl.ANY); sm=pl.BlockSpec(memory_space=pltpu.SMEM)
    return pl.pallas_call(pick_body,out_shape=(jax.ShapeDtypeStruct((PAY,128),B),)*3,
      in_specs=[sm,sm,an],out_specs=(an,)*3,
      scratch_shapes=[pltpu.VMEM((4,ROWS,128),B),pltpu.VMEM((3,16,128),B),pltpu.SemaphoreType.DMA((4,)),pltpu.SemaphoreType.DMA((9,))],
      compiler_params=pltpu.CompilerParams(vmem_limit_bytes=12<<20),
      cost_estimate=pl.CostEstimate(flops=0,bytes_accessed=6<<20,transcendentals=0),
      name='pick')(tab,me,pre)

def place_body(tab,me_ref,src,r1,r3,r2,out,buf,zero,isem,osem):
    me=me_ref[0]
    used=jnp.int32(0)
    for b in range(4):
        hit=(tab[b]>>3)==me
        slot=tab[b]&7
        @pl.when(hit)
        def _(b=b,slot=slot):
            pltpu.make_async_copy(src.at[pl.ds(b*ROWS,ROWS),:],buf.at[slot],isem.at[slot]).start()
        used=used|jnp.where(hit,jnp.int32(1)<<slot,0)
    here=used
    for ref,on in ((r1,True),(r3,True),(r2,True)):
        lab=ref[2*ROWS:2*ROWS+16,:].astype(F)
        for s in range(2):
            v=jnp.max(lab[s*8:s*8+8]).astype(jnp.int32)
            hit=(v>=0)&on
            slot=v&7
            @pl.when(hit)
            def _(ref=ref,s=s,slot=slot):
                pltpu.make_async_copy(ref.at[pl.ds(s*ROWS,ROWS),:],out.at[slot],osem.at[slot]).start()
            used=used|jnp.where(hit,jnp.int32(1)<<slot,0)
    zero[...]=jnp.zeros_like(zero)
    for s in range(8):
        @pl.when(((used>>s)&1)==0)
        def _(s=s):
            pltpu.make_async_copy(zero,out.at[s],osem.at[s]).start()
    for s in range(8):
        @pl.when(((here>>s)&1)==1)
        def _(s=s):
            pltpu.make_async_copy(src.at[pl.ds(0,ROWS),:],buf.at[s],isem.at[s]).wait()
            pltpu.make_async_copy(buf.at[s],out.at[s],osem.at[s]).start()
    for s in range(8):
        pltpu.make_async_copy(zero,out.at[s],osem.at[s]).wait()

def place(tab,me,pre,*got):
    an=pl.BlockSpec(memory_space=pl.ANY); sm=pl.BlockSpec(memory_space=pltpu.SMEM); vm=pl.BlockSpec(memory_space=pltpu.VMEM)
    return pl.pallas_call(place_body,out_shape=jax.ShapeDtypeStruct((8,ROWS,128),B),
      in_specs=[sm,sm,an,vm,vm,vm],out_specs=an,
      scratch_shapes=[pltpu.VMEM((8,ROWS,128),B),pltpu.VMEM((ROWS,128),B),
        pltpu.SemaphoreType.DMA((8,)),pltpu.SemaphoreType.DMA((8,))],
      compiler_params=pltpu.CompilerParams(vmem_limit_bytes=12<<20),
      cost_estimate=pl.CostEstimate(flops=0,bytes_accessed=8<<20,transcendentals=0),
      name='place')(tab,me,pre,*got)

def ahead(value,steps):
    return lax.ppermute(value,"page",[(s,(s+steps)%64) for s in range(64)])

def swap(value):
    return lax.ppermute(value,"head",[(0,1),(1,0)])

def body(streams,hc_read,hc_carry,hc_write,w_qkv,w_out,req_lengths,req_age,cache_order,cache_kv,prefill_kv,page_table):
    head=lax.axis_index("head").astype(jnp.int32).reshape(1)
    me=lax.axis_index("page").astype(jnp.int32).reshape(1)
    lens=req_lengths[0]; age=req_age[0]; order=cache_order[0]
    x=rows_view(streams)
    own0=mix(0,x,hc_read)
    oth0=swap(own0)
    x1,own0=lax.optimization_barrier((x,own0))
    own1=mix(1,x1,hc_read)
    oth1=swap(own1)
    pre=tiles_view(prefill_kv.reshape(1024,1024))
    own_dep,table=lax.optimization_barrier((own1,page_table))
    s1,s2,s3=pick(table,me,pre)
    r3=ahead(s3,3); r1=ahead(s1,1)
    cos,sin=tables(lens,age)
    wq,wk,wv,kc,vc=prep(order,w_qkv.transpose(1,0,2),cache_kv)
    oth1,s2,wq,wk,wv,kc,vc=lax.optimization_barrier((oth1,s2,wq,wk,wv,kc,vc))
    r2=ahead(s2,2)
    q,k,v=proj(head,own0,own1,oth0,oth1,cos,sin,wq,wk,wv)
    parts=attn(lens,age,head,q,k,v,kc,vc,w_out)
    keeps,sends=list(parts[:NF]),list(parts[NF:])
    recvs=[swap(s) for s in sends]
    carry=(jnp.eye(4,dtype=F)+hc_carry).reshape(16)
    xd,_=lax.optimization_barrier((x,keeps[0]))
    ready=warm(xd,carry,hc_write)
    pages=place(page_table,me,pre,r1,r3,r2)
    ready,recvs[0],pages=lax.optimization_barrier((ready,recvs[0],pages))
    new=None
    for i in range(NF): new=fin(i,ready,keeps[i],recvs[i],new)
    return rows_unview(new),tiles_unview(pages.reshape(8*ROWS,128)).reshape(8,1,2,128,1024)

def solution(mesh):
    placed=(P("page",None,"head"),P(),P(),P(),P(None,None,"head"),P("head",None),P("page",None),P("page",None),P("page",None),
        P("page",None,None,"head"),P("page",None,None,None,"head"),P("page"))
    return jax.shard_map(body,mesh=mesh,in_specs=placed,out_specs=(P("page",None,"head"),P("page",None,None,None,"head")),check_vma=False)
```

```python
import functools
import math

import jax
import jax.numpy as jnp
from jax import lax
from jax.experimental import pallas as pl
from jax.experimental.pallas import tpu as pltpu
from jax.sharding import PartitionSpec as P

F=jnp.float32; B=jnp.bfloat16
NEG=-1e30
def io(shape,d): return lax.broadcasted_iota(jnp.int32,shape,d)
def dot_t(a,b): return lax.dot_general(a,b,(((1,),(1,)),((),())),preferred_element_type=F)
def dot(a,b): return jnp.dot(a,b,preferred_element_type=F)
QSCALE=math.log2(math.e)/math.sqrt(128.0)

def proj_body(head_ref,own0,own1,oth0,oth1,cos_ref,sin_ref,wq,wk,wv,q,k,v,nrm):
    h=head_ref[0]
    hoff=pl.multiple_of(h*1024,1024); ooff=pl.multiple_of((1-h)*1024,1024)
    for half,(own_ref,oth_ref) in enumerate(((own0,oth0),(own1,oth1))):
        def ln(i,_,half=half,own_ref=own_ref,oth_ref=oth_ref):
            r=pl.ds(pl.multiple_of(i*16,16),16)
            o=pl.ds(pl.multiple_of(HEADCUT[half]+i*16,16),16)
            a=own_ref[r,:].astype(F); b=oth_ref[r,:].astype(F)
            m=jnp.sum(a+b,axis=1,keepdims=True)*(1.0/2048)
            a=a-m; b=b-m
            var=jnp.sum(a*a+b*b,axis=1,keepdims=True)*(1.0/2048)
            rs=lax.rsqrt(var+1e-5)
            nrm[o,pl.ds(hoff,1024)]=(a*rs).astype(B)
            nrm[o,pl.ds(ooff,1024)]=(b*rs).astype(B)
            return 0
        lax.fori_loop(0,(HEADCUT[half+1]-HEADCUT[half])//16,ln,0,unroll=8)
    for c,dst,w in ((0,q,wq),(1,k,wk),(2,v,wv)):
        def proj(i,_,c=c,dst=dst,w=w):
            col=pl.ds(pl.multiple_of(i*256,256),256)
            for rb in range(2):
                rows=slice(rb*256,rb*256+256)
                x=dot(nrm[rows,:],w[:,col])
                if c<2:
                    co=cos_ref[rows,:]; si=sin_ref[rows,:]
                    y=[]
                    for hh in range(2):
                        xh=x[:,hh*128:hh*128+128]
                        z=xh*co+pltpu.roll(xh,64,1)*si
                        if c==0: z=z*QSCALE
                        y.append(z)
                    x=jnp.concatenate(y,axis=1)
                dst[rows,col]=x.astype(B)
            return 0
        lax.fori_loop(0,4,proj,0)

def proj(head,own0,own1,oth0,oth1,cos,sin,wq,wk,wv):
    vm=pl.BlockSpec(memory_space=pltpu.VMEM); sm=pl.BlockSpec(memory_space=pltpu.SMEM)
    return pl.pallas_call(proj_body,out_shape=(jax.ShapeDtypeStruct((512,1024),B),)*3,
        in_specs=[sm]+[vm]*9,out_specs=(vm,)*3,scratch_shapes=[pltpu.VMEM((512,2048),B)],
        compiler_params=pltpu.CompilerParams(vmem_limit_bytes=12<<20),
        cost_estimate=pl.CostEstimate(flops=7*10**9,bytes_accessed=16<<20,transcendentals=0),
        name='proj')(head,own0,own1,oth0,oth1,cos,sin,wq,wk,wv)

def attn_body(len_ref,age_ref,head_ref,q,k,v,kc,vc,wo_hbm,*rest):
    keeps=rest[:NF]; sends=rest[NF:2*NF]
    (wo,att,s_ref,p_ref,acc,wosem)=rest[2*NF:]
    wocp=pltpu.make_async_copy(wo_hbm,wo,wosem)
    wocp.start()
    h=head_ref[0]
    hoff=pl.multiple_of(h*1024,1024); ooff=pl.multiple_of((1-h)*1024,1024)
    e=[len_ref[0],len_ref[0]+len_ref[1],len_ref[0]+len_ref[1]+len_ref[2]]
    def tile(t,_):
        t0=t*128
        rows=pl.ds(pl.multiple_of(t0,128),128)
        kb=jnp.maximum(t-2,0)*128
        win=pl.ds(pl.multiple_of(kb,128),384)
        ri=t0+io((128,384),0); ki=kb+io((128,384),1)
        st=jnp.where(ri>=e[2],e[2],jnp.where(ri>=e[1],e[1],jnp.where(ri>=e[0],e[0],0)))
        bias=jnp.where((ki>=st)&(ki<=ri),0.0,NEG)
        for hh in range(8):
            hs=slice(hh*128,hh*128+128)
            s_ref[hh,:,384:768]=dot_t(q[rows,hs],k[win,hs])+bias
        rid=t0+io((128,1),0)
        rreq=(rid>=e[0]).astype(jnp.int32)+(rid>=e[1]).astype(jnp.int32)+(rid>=e[2]).astype(jnp.int32)
        last=t0+127
        lo=(t0>=e[0]).astype(jnp.int32)+(t0>=e[1]).astype(jnp.int32)+(t0>=e[2]).astype(jnp.int32)
        hi=(last>=e[0]).astype(jnp.int32)+(last>=e[1]).astype(jnp.int32)+(last>=e[2]).astype(jnp.int32)
        def sc(r,_):
            cb=jnp.where(io((1,384),1)<age_ref[r],0.0,NEG)
            keys=pl.ds(pl.multiple_of(r*384,384),384)
            mine=rreq==r
            for hh in range(8):
                hs=slice(hh*128,hh*128+128)
                x=dot_t(q[rows,hs],kc[keys,hs])+cb
                s_ref[hh,:,0:384]=jnp.where(mine,x,s_ref[hh,:,0:384])
            return 0
        lax.fori_loop(lo,hi+1,sc,0)
        for hh in range(8):
            hs=slice(hh*128,hh*128+128)
            s=s_ref[hh]
            m=jnp.max(s,axis=1,keepdims=True)
            p=jnp.exp2(s-m)
            l=jnp.sum(p,axis=1,keepdims=True)
            p=(p*(1.0/l)).astype(B)
            p_ref[hh]=p[:,0:384]
            acc[:,hs]=dot(p[:,384:768],v[win,hs])
        def pv(r,_):
            keys=pl.ds(pl.multiple_of(r*384,384),384)
            mine=rreq==r
            for hh in range(8):
                hs=slice(hh*128,hh*128+128)
                pm=jnp.where(mine,p_ref[hh],jnp.zeros((),B))
                acc[:,hs]=acc[:,hs]+dot(pm,vc[keys,hs])
            return 0
        lax.fori_loop(lo,hi+1,pv,0)
        att[rows,:]=acc[...].astype(B)
        return 0
    lax.fori_loop(0,4,tile,0)
    wocp.wait()
    def outp(i,_):
        lc=pl.multiple_of(i*256,256)
        for rb in range(4):
            rows=slice(rb*128,rb*128+128)
            p=max(i for i in range(NF) if CUTS[i]<=rb*128)
            to=slice(rb*128-CUTS[p],rb*128-CUTS[p]+128)
            for dst,off in ((sends[p],ooff),(keeps[p],hoff)):
                dst[to,pl.ds(lc,256)]=dot(att[rows,:],wo[:,pl.ds(pl.multiple_of(off+lc,256),256)]).astype(B)
        return 0
    lax.fori_loop(0,4,outp,0)

def attn(lens,age,head,q,k,v,kc,vc,wo):
    vm=pl.BlockSpec(memory_space=pltpu.VMEM); an=pl.BlockSpec(memory_space=pl.ANY); sm=pl.BlockSpec(memory_space=pltpu.SMEM)
    return pl.pallas_call(attn_body,
        out_shape=tuple(jax.ShapeDtypeStruct((CUTS[i+1]-CUTS[i],1024),B) for i in range(NF))*2,
        in_specs=[sm]*3+[vm]*5+[an], out_specs=(vm,)*(2*NF),
        scratch_shapes=[pltpu.VMEM((1024,2048),B),pltpu.VMEM((512,1024),B),
            pltpu.VMEM((8,128,768),F),pltpu.VMEM((8,128,384),B),pltpu.VMEM((128,1024),F),pltpu.SemaphoreType.DMA],
        compiler_params=pltpu.CompilerParams(vmem_limit_bytes=40<<20),
        cost_estimate=pl.CostEstimate(flops=7*10**9,bytes_accessed=16<<20,transcendentals=4<<20),
        name='attn')(lens,age,head,q,k,v,kc,vc,wo)

def prep_body(order_ref,w_hbm,kv_hbm,wq,wk,wv,kc,vc,wsem,csem):
    cps=[pltpu.make_async_copy(w_hbm.at[c],w,wsem.at[c]) for c,w in enumerate((wq,wk,wv))]
    for i in range(12):
        pg=order_ref[i]
        cps.append(pltpu.make_async_copy(kv_hbm.at[pg,0],kc.at[pl.ds(i*128,128),:],csem.at[2*i]))
        cps.append(pltpu.make_async_copy(kv_hbm.at[pg,1],vc.at[pl.ds(i*128,128),:],csem.at[2*i+1]))
    for c in cps: c.start()
    for c in cps: c.wait()

def prep(order,w3,kv):
    vm=pl.BlockSpec(memory_space=pltpu.VMEM); an=pl.BlockSpec(memory_space=pl.ANY); sm=pl.BlockSpec(memory_space=pltpu.SMEM)
    return pl.pallas_call(prep_body,
        out_shape=tuple(jax.ShapeDtypeStruct(s,B) for s in ((2048,1024),)*3+((1536,1024),)*2),
        in_specs=[sm,an,an],out_specs=(vm,)*5,
        scratch_shapes=[pltpu.SemaphoreType.DMA((3,)),pltpu.SemaphoreType.DMA((24,))],
        compiler_params=pltpu.CompilerParams(vmem_limit_bytes=30<<20),
        cost_estimate=pl.CostEstimate(flops=0,bytes_accessed=46<<20,transcendentals=0),
        name='prep')(order,w3,kv)

def tables(lens,age):
    ends=jnp.cumsum(lens); starts=ends-lens
    t=jnp.arange(512,dtype=jnp.int32)
    mem=((t[:,None]>=starts[None,:])&(t[:,None]<ends[None,:])).astype(jnp.int32)
    pos=t+jnp.sum(mem*(age-starts)[None,:],axis=1)
    j=jnp.arange(128,dtype=jnp.int32)
    freq=10000.0**(-2.0*(j%64).astype(F)/128)
    ang=pos.astype(F)[:,None]*freq[None,:]
    return jnp.cos(ang), jnp.where(j[None,:]<64,-1.0,1.0)*jnp.sin(ang)

def rows_view(x):
    return x.reshape(512,4,8,128).transpose(0,2,1,3).reshape(16384,128)

def rows_unview(x):
    return x.reshape(512,8,4,128).transpose(0,2,1,3).reshape(512,4,1024)

HEADCUT=(0,128,512)
TCH=64

def mix_body(base,size,r_ref,x_hbm,o_ref,x,sem):
    NCH=size//TCH
    cps=[pltpu.make_async_copy(x_hbm.at[pl.ds(base*32+c*TCH*32,TCH*32),:],x.at[pl.ds(c*TCH*32,TCH*32),:],sem.at[c]) for c in range(NCH)]
    for c in cps: c.start()
    sh=(64,256); row=io(sh,0); col=io(sh,1)
    c=col&3
    a=jnp.where(c==0,r_ref[0],jnp.where(c==1,r_ref[1],jnp.where(c==2,r_ref[2],r_ref[3])))
    a=jnp.where(((col>>5)==(row&7))&(((col>>2)&7)==(row>>3)),a,0.0)
    hi=a.astype(B)
    A=jnp.concatenate([hi,(a-hi.astype(F)).astype(B)],axis=0)
    for ch in range(NCH):
        cps[ch].wait()
        for g in range(ch*TCH//16,(ch+1)*TCH//16):
            X=jnp.concatenate([x[g*512:g*512+256,:],x[g*512+256:g*512+512,:]],axis=1)
            o=dot(A,X)
            o=o[0:64]+o[64:128]
            for j in range(8):
                o_ref[g*16:g*16+16,j*128:(j+1)*128]=jnp.concatenate([o[j*8:j*8+8,0:128],o[j*8:j*8+8,128:256]],axis=0).astype(B)

def mix(i,x,r):
    base,MR=HEADCUT[i],HEADCUT[i+1]-HEADCUT[i]
    return pl.pallas_call(functools.partial(mix_body,base,MR),out_shape=jax.ShapeDtypeStruct((MR,1024),B),
      in_specs=[pl.BlockSpec(memory_space=pltpu.SMEM),pl.BlockSpec(memory_space=pl.ANY)],
      out_specs=pl.BlockSpec(memory_space=pltpu.VMEM),
      scratch_shapes=[pltpu.VMEM((MR*32,128),B),pltpu.SemaphoreType.DMA((MR//TCH,))],
      compiler_params=pltpu.CompilerParams(vmem_limit_bytes=61<<20),
      cost_estimate=pl.CostEstimate(flops=10**8,bytes_accessed=3<<20,transcendentals=0),
      name='mix')(r,x)

CUTS=(0,384,512)
NF=2
STEP=32

def warm_body(c_ref,w_ref,x_hbm,x,m_ref,wm_ref,sem):
    cp=pltpu.make_async_copy(x_hbm,x,sem)
    cp.start()
    n=128
    row=io((n,n),0); col=io((n,n),1)
    a=jnp.zeros((n,n),F)
    for i in range(4):
        for j in range(4):
            a=jnp.where(((row&3)==j)&((col&3)==i),c_ref[i*4+j],a)
    a=jnp.where((row>>2)==(col>>2),a,0.0)
    hi=a.astype(B); m_ref[:,0:n]=hi; m_ref[:,n:2*n]=(a-hi.astype(F)).astype(B)
    for s in range(2):
        row=io((n,64),0); col=io((n,64),1)
        a=jnp.zeros((n,64),F)
        for j in range(4): a=jnp.where((row&3)==j,w_ref[j],a)
        a=jnp.where(((row>>5)+s*4==(col&7))&(((row>>2)&7)==(col>>3)),a,0.0)
        hi=a.astype(B); lo=(a-hi.astype(F)).astype(B)
        wm_ref[s*n:(s+1)*n,:]=jnp.concatenate([hi,lo,hi,lo],axis=1)
    cp.wait()

def warm(x,cr,w):
    an=pl.BlockSpec(memory_space=pl.ANY); sm=pl.BlockSpec(memory_space=pltpu.SMEM); vm=pl.BlockSpec(memory_space=pltpu.VMEM)
    return pl.pallas_call(warm_body,
      out_shape=(jax.ShapeDtypeStruct((16384,128),B),jax.ShapeDtypeStruct((128,256),B),jax.ShapeDtypeStruct((256,256),B)),
      in_specs=[sm,sm,an],out_specs=(vm,)*3,scratch_shapes=[pltpu.SemaphoreType.DMA],
      compiler_params=pltpu.CompilerParams(vmem_limit_bytes=48<<20),
      cost_estimate=pl.CostEstimate(flops=0,bytes_accessed=8<<20,transcendentals=0),
      name='warm')(cr,w,x)

def fin_body(base,size,x,m_ref,wm_ref,a_ref,b_ref,*rest):
    o_hbm,o,osem=rest[-3:]
    FCH=size//STEP
    ocp=[pltpu.make_async_copy(o.at[pl.ds(c*STEP*32,STEP*32),:],o_hbm.at[pl.ds((base+c*STEP)*32,STEP*32),:],osem.at[c]) for c in range(FCH)]
    M=m_ref[...]
    for ch in range(FCH):
        for g in range(ch*STEP//16,(ch+1)*STEP//16):
            def U(ref):
                u=ref[g*16:g*16+16,:].astype(F)
                return jnp.concatenate([jnp.concatenate([u[0:8,j*128:(j+1)*128],u[8:16,j*128:(j+1)*128]],axis=1) for j in range(8)],axis=0).astype(B)
            Ua=U(a_ref);Ub=U(b_ref)
            ou=dot(wm_ref[...],jnp.concatenate([Ua,Ua,Ub,Ub],axis=0))
            r0=g*512; q0=base*32+r0
            for s in range(2):
                X=jnp.concatenate([x[q0+s*128:q0+s*128+128,:],x[q0+256+s*128:q0+256+s*128+128,:]],axis=1)
                z=(dot(M,jnp.concatenate([X,X],axis=0))+ou[s*128:(s+1)*128]).astype(B)
                o[r0+s*128:r0+s*128+128,:]=z[:,0:128]; o[r0+256+s*128:r0+256+s*128+128,:]=z[:,128:256]
        ocp[ch].start()
    for c in ocp: c.wait()

def fin(i,ready,u1,u2,prev):
    an=pl.BlockSpec(memory_space=pl.ANY); vm=pl.BlockSpec(memory_space=pltpu.VMEM)
    more=[] if prev is None else [prev]
    base,size=CUTS[i],CUTS[i+1]-CUTS[i]
    return pl.pallas_call(functools.partial(fin_body,base,size),out_shape=jax.ShapeDtypeStruct((16384,128),B),
      in_specs=[vm]*5+[an]*len(more),out_specs=an,
      scratch_shapes=[pltpu.VMEM((size*32,128),B),pltpu.SemaphoreType.DMA((size//STEP,))],
      input_output_aliases={5:0} if more else {},
      compiler_params=pltpu.CompilerParams(vmem_limit_bytes=16<<20),
      cost_estimate=pl.CostEstimate(flops=10**9*size//512,bytes_accessed=(10<<20)*size//512,transcendentals=0),
      name='fin')(*ready,u1,u2,*more)

ROWS=2048
PAY=2*ROWS+16

def tiles_view(x):
    n=x.shape[0]
    return x.reshape(n//8,8,8,128).transpose(0,2,1,3).reshape(n*8,128)

def tiles_unview(x):
    n=x.shape[0]//8
    return x.reshape(n//8,8,8,128).transpose(0,2,1,3).reshape(n,1024)

def pick_body(tab_ref,me_ref,src,o1,o2,o3,buf,lab,isem,osem):
    me=me_ref[0]
    icp=[pltpu.make_async_copy(src.at[pl.ds(b*ROWS,ROWS),:],buf.at[b],isem.at[b]) for b in range(4)]
    for c in icp: c.start()
    plan=[]
    for d,dst in ((3,o3),(2,o2),(1,o1)):
        cnt=jnp.int32(0); i=[jnp.int32(0)]*2; l=[jnp.int32(-1)]*2
        for b in range(4):
            hit=(((tab_ref[b]>>3)-me)&63)==d
            for s in range(2):
                i[s]=jnp.where(hit&(cnt==s),b,i[s])
                l[s]=jnp.where(hit&(cnt==s),tab_ref[b]&7,l[s])
            cnt=cnt+hit.astype(jnp.int32)
        lab[d-1]=jnp.where(io((16,128),0)<8,l[0].astype(F),l[1].astype(F)).astype(B)
        plan.append((d,dst,i))
    for c in icp: c.wait()
    cps=[]
    for d,dst,i in plan:
        for s in range(2):
            cps.append(pltpu.make_async_copy(buf.at[i[s]],dst.at[pl.ds(s*ROWS,ROWS),:],osem.at[3*(d-1)+s]))
        cps.append(pltpu.make_async_copy(lab.at[d-1],dst.at[pl.ds(2*ROWS,16),:],osem.at[3*(d-1)+2]))
    for c in cps: c.start()
    for c in cps: c.wait()

def pick(tab,me,pre):
    an=pl.BlockSpec(memory_space=pl.ANY); sm=pl.BlockSpec(memory_space=pltpu.SMEM)
    return pl.pallas_call(pick_body,out_shape=(jax.ShapeDtypeStruct((PAY,128),B),)*3,
      in_specs=[sm,sm,an],out_specs=(an,)*3,
      scratch_shapes=[pltpu.VMEM((4,ROWS,128),B),pltpu.VMEM((3,16,128),B),pltpu.SemaphoreType.DMA((4,)),pltpu.SemaphoreType.DMA((9,))],
      compiler_params=pltpu.CompilerParams(vmem_limit_bytes=12<<20),
      cost_estimate=pl.CostEstimate(flops=0,bytes_accessed=6<<20,transcendentals=0),
      name='pick')(tab,me,pre)

def place_body(tab,me_ref,src,r1,r3,r2,out,buf,zero,isem,osem):
    me=me_ref[0]
    used=jnp.int32(0)
    for b in range(4):
        hit=(tab[b]>>3)==me
        slot=tab[b]&7
        @pl.when(hit)
        def _(b=b,slot=slot):
            pltpu.make_async_copy(src.at[pl.ds(b*ROWS,ROWS),:],buf.at[slot],isem.at[slot]).start()
        used=used|jnp.where(hit,jnp.int32(1)<<slot,0)
    here=used
    for ref,on in ((r1,True),(r3,True),(r2,True)):
        lab=ref[2*ROWS:2*ROWS+16,:].astype(F)
        for s in range(2):
            v=jnp.max(lab[s*8:s*8+8]).astype(jnp.int32)
            hit=(v>=0)&on
            slot=v&7
            @pl.when(hit)
            def _(ref=ref,s=s,slot=slot):
                pltpu.make_async_copy(ref.at[pl.ds(s*ROWS,ROWS),:],out.at[slot],osem.at[slot]).start()
            used=used|jnp.where(hit,jnp.int32(1)<<slot,0)
    zero[...]=jnp.zeros_like(zero)
    for s in range(8):
        @pl.when(((used>>s)&1)==0)
        def _(s=s):
            pltpu.make_async_copy(zero,out.at[s],osem.at[s]).start()
    for s in range(8):
        @pl.when(((here>>s)&1)==1)
        def _(s=s):
            pltpu.make_async_copy(src.at[pl.ds(0,ROWS),:],buf.at[s],isem.at[s]).wait()
            pltpu.make_async_copy(buf.at[s],out.at[s],osem.at[s]).start()
    for s in range(8):
        pltpu.make_async_copy(zero,out.at[s],osem.at[s]).wait()

def place(tab,me,pre,*got):
    an=pl.BlockSpec(memory_space=pl.ANY); sm=pl.BlockSpec(memory_space=pltpu.SMEM); vm=pl.BlockSpec(memory_space=pltpu.VMEM)
    return pl.pallas_call(place_body,out_shape=jax.ShapeDtypeStruct((8,ROWS,128),B),
      in_specs=[sm,sm,an,vm,vm,vm],out_specs=an,
      scratch_shapes=[pltpu.VMEM((8,ROWS,128),B),pltpu.VMEM((ROWS,128),B),
        pltpu.SemaphoreType.DMA((8,)),pltpu.SemaphoreType.DMA((8,))],
      compiler_params=pltpu.CompilerParams(vmem_limit_bytes=12<<20),
      cost_estimate=pl.CostEstimate(flops=0,bytes_accessed=8<<20,transcendentals=0),
      name='place')(tab,me,pre,*got)

def ahead(value,steps):
    return lax.ppermute(value,"page",[(s,(s+steps)%64) for s in range(64)])

def swap(value):
    return lax.ppermute(value,"head",[(0,1),(1,0)])

def body(streams,hc_read,hc_carry,hc_write,w_qkv,w_out,req_lengths,req_age,cache_order,cache_kv,prefill_kv,page_table):
    head=lax.axis_index("head").astype(jnp.int32).reshape(1)
    me=lax.axis_index("page").astype(jnp.int32).reshape(1)
    lens=req_lengths[0]; age=req_age[0]; order=cache_order[0]
    x=rows_view(streams)
    own0=mix(0,x,hc_read)
    oth0=swap(own0)
    x1,own0=lax.optimization_barrier((x,own0))
    own1=mix(1,x1,hc_read)
    oth1=swap(own1)
    pre=tiles_view(prefill_kv.reshape(1024,1024))
    own_dep,table=lax.optimization_barrier((own1,page_table))
    s1,s2,s3=pick(table,me,pre)
    r2=ahead(s2,2); r3=ahead(s3,3); r1=ahead(s1,1)
    cos,sin=tables(lens,age)
    wq,wk,wv,kc,vc=prep(order,w_qkv.transpose(1,0,2),cache_kv)
    oth1,wq,wk,wv,kc,vc=lax.optimization_barrier((oth1,wq,wk,wv,kc,vc))
    q,k,v=proj(head,own0,own1,oth0,oth1,cos,sin,wq,wk,wv)
    parts=attn(lens,age,head,q,k,v,kc,vc,w_out)
    keeps,sends=list(parts[:NF]),list(parts[NF:])
    recvs=[swap(s) for s in sends]
    carry=(jnp.eye(4,dtype=F)+hc_carry).reshape(16)
    xd,_=lax.optimization_barrier((x,keeps[0]))
    ready=warm(xd,carry,hc_write)
    pages=place(page_table,me,pre,r1,r3,r2)
    ready,recvs[0],pages=lax.optimization_barrier((ready,recvs[0],pages))
    new=None
    for i in range(NF): new=fin(i,ready,keeps[i],recvs[i],new)
    return rows_unview(new),tiles_unview(pages.reshape(8*ROWS,128)).reshape(8,1,2,128,1024)

def solution(mesh):
    placed=(P("page",None,"head"),P(),P(),P(),P(None,None,"head"),P("head",None),P("page",None),P("page",None),P("page",None),
        P("page",None,None,"head"),P("page",None,None,None,"head"),P("page"))
    return jax.shard_map(body,mesh=mesh,in_specs=placed,out_specs=(P("page",None,"head"),P("page",None,None,None,"head")),check_vma=False)
```
